128 devices in a mesh: dev: 128 (over x, z, y, core).
Axes of the slice: x: 4, y: 4, z: 4, core: 2. Of those that a mesh axis runs over, the one named last changes fastest.
Arguments:
- saved: bfloat16 [128, 1024, 768], P('dev'), may hold values from -6 to 6
- cotangent: bfloat16 [128, 1024, 2048], P('dev'), may hold values from -6 to 6
- weights: bfloat16 [128, 768, 2048], P('dev'), may hold values from -0.21875 to 0.21875
- counts: int32 [64], replicated, may hold values from 1 to 8, as said below
- live_rows: int32 [128], P('dev'), may hold values from 1 to 1024, 81920 in all
- next_map: int32 [128], replicated, may hold values from 0 to 63, as said below
- master: float32 [64, 768, 2048], P(None, 'dev'), may hold values from -0.21875 to 0.21875
- moment1: bfloat16 [64, 768, 2048], P(None, 'dev'), may hold values from -6 to 6
- moment2: bfloat16 [64, 768, 2048], P(None, 'dev'), may hold values from 0.049804688 to 4
Outputs:
- input_grads: bfloat16 [128, 1024, 768], P('dev')
- master_out: float32 [64, 768, 2048], P(None, 'dev')
- moment1_out: bfloat16 [64, 768, 2048], P(None, 'dev')
- moment2_out: bfloat16 [64, 768, 2048], P(None, 'dev')
- next_weights: bfloat16 [128, 768, 2048], P('dev')
The draws below stay inside these ranges and needn't reach their ends.
Inputs may be any that keep to these rules, and one draw needn't show every extreme that they name: The counts sum to 128; in the current placement expert e holds the counts[e] slots that follow those of experts below e; some expert has exactly 8 replicas. `next_map`: every expert is named by 1 to 8 slots; some expert by exactly 8. `live_rows`: the live rows of all slots sum to 81920, and some slot has exactly 1024.
All inputs are finite; a program needn't handle non-finite values. No bound on the sum of `live_rows` on one device may be relied on, other than what follows from the above.
Results may differ from the reference program's by a relative error of at most 0.0058.
Values may be sent and summed in bfloat16 or wider, within the bound.
No kernel may reach another device: no remote copies, remote signals or barrier semaphores. Data moves between devices by JAX's collectives and lax.ppermute only.
A program may use at most 128 MiB of HBM per device.

```python
import math
import jax
import jax.numpy as jnp
import numpy as np
from jax import lax

D = 2048
HID = 768
ROWS = 1024
SLOTS = 128
EXPERTS = 64


def replica_counts(key):
    shuffled = jax.random.permutation(jax.random.fold_in(key, 1), EXPERTS).astype(jnp.int32)
    ranking = jnp.zeros((EXPERTS,), jnp.int32).at[shuffled].set(jnp.arange(EXPERTS, dtype=jnp.int32))
    initial = jnp.ones((EXPERTS,), jnp.int32).at[shuffled[0]].set(8)

    def place(number, current):
        priority = jax.random.randint(jax.random.fold_in(key, 100 + number), (EXPERTS,), 0, 1 << 20) // (1 + ranking)
        priority = jnp.where((current < 8) & (ranking > 0), priority, -1)
        return current.at[jnp.argmax(priority)].add(1)
    return lax.fori_loop(0, SLOTS - EXPERTS - 7, place, initial)


def draw_counts(key, part):
    return replica_counts(jax.random.fold_in(key, 11)).astype(jnp.int32)


def draw_next_map(key, part):
    tally = replica_counts(jax.random.fold_in(key, 22))
    bounds = jnp.cumsum(tally)
    slot_index = jnp.arange(SLOTS, dtype=jnp.int32)
    owners = jnp.sum((bounds[None, :] <= slot_index[:, None]).astype(jnp.int32), axis=1)
    shuffle = jax.random.permutation(jax.random.fold_in(key, 33), SLOTS)
    return owners[shuffle].astype(jnp.int32)


def levels(key, shape, pieces, least, largest):
    def one(position, blocks):
        heights = jax.random.uniform(jax.random.fold_in(jax.random.fold_in(key, 6), position), (blocks,), jnp.float32, least / len(pieces), largest / len(pieces))
        return jnp.repeat(jnp.exp(heights), shape[position] // blocks).reshape((-1,) + (1,) * (len(shape) - position - 1))

    level = one(*pieces[0])
    for cut in pieces[1:]:
        level = level * one(*cut)
    return level


def profile(amount, total, most, slope):
    loads = [(1 << 20) // math.isqrt(rank ** slope) + 1 for rank in range(2, amount + 1)]
    rest, given = total - most - (amount - 1), [1] * (amount - 1)
    while rest > 0:
        candidates = [i for i in range(amount - 1) if given[i] < most]
        pool, remaining = sum([loads[i] for i in candidates]), rest
        for i in candidates:
            extra = min(most - given[i], max(1, remaining * loads[i] // pool), rest)
            given[i] = given[i] + extra
            rest = rest - extra
    return np.array([most] + given)


def ragged_sizes(key, number_of, total, reach, skew):
    if number_of == 2:
        one = jax.random.randint(key, (), max(1, total - reach), min(reach, total - 1) + 1)
        return jnp.stack([one, total - one])
    lengths = jnp.asarray(profile(number_of, total, reach, skew), jnp.int32)
    couples = (number_of - 1) // 2
    source_of, sink = lengths[1:1 + 2 * couples:2], lengths[2:2 + 2 * couples:2]
    slack = jnp.minimum(source_of - 1, reach - sink)
    passed = jax.random.randint(jax.random.fold_in(key, 1), (couples,), 0, 1 << 20) % (slack + 1)
    lengths = lengths.at[1:1 + 2 * couples:2].set(source_of - passed).at[2:2 + 2 * couples:2].set(sink + passed)
    return lengths[jax.random.permutation(jax.random.fold_in(key, 2), number_of)]


def bell_draw(key, extent, deviation, reach, pieces=(), kind=jnp.bfloat16):
    values = deviation * jax.random.normal(key, extent, jnp.float32)
    if pieces:
        values = values * levels(key, extent, pieces, -0.22, 0.18)
    return jnp.clip(values, -reach, reach).astype(kind)


def setup_inputs(seed: int = 0) -> dict:
    streams_of = jax.random.split(jax.random.key(seed), 10)
    saved = bell_draw(streams_of[0], (SLOTS, ROWS, HID), 1.0, 6.0, ((0, 128),))
    cotangent = bell_draw(streams_of[1], (SLOTS, ROWS, D), 1.0, 6.0, ((0, 128),))
    weights = bell_draw(streams_of[2], (SLOTS, HID, D), HID ** -0.5, 0.21875, ((0, 128),))
    counts = draw_counts(jax.random.fold_in(streams_of[9], 71), 0)
    live_rows = ragged_sizes(streams_of[4], SLOTS, SLOTS * ROWS * 5 // 8, ROWS, 2).astype(jnp.int32)
    next_map = draw_next_map(jax.random.fold_in(streams_of[9], 71), 0)
    master = bell_draw(streams_of[6], (EXPERTS, HID, D), HID ** -0.5, 0.21875, ((1, 128),), jnp.float32)
    moment1 = bell_draw(streams_of[7], (EXPERTS, HID, D), 1.0, 6.0, ((1, 128),))
    moment2 = jnp.clip(jnp.exp(math.log(4.0) - 4.3859405 * jax.random.uniform(streams_of[8], (EXPERTS, HID, D), jnp.float32) ** levels(streams_of[8], (EXPERTS, HID, D), ((1, 128),), -0.2, 0.2)), 0.049804688, 4.0).astype(jnp.bfloat16)
    return dict(saved=saved, cotangent=cotangent, weights=weights, counts=counts, live_rows=live_rows, next_map=next_map, master=master, moment1=moment1, moment2=moment2)


LEARN_RATE = 0.001
DECAY_RATE = 0.1
BETA_ONE = 0.9
BETA_TWO = 0.95
BIAS_ONE = 1.0 - 0.9 ** 20
BIAS_TWO = 1.0 - 0.95 ** 20
EPSILON = 1e-08

def reference(saved, cotangent, weights, counts, live_rows, next_map, master, moment1, moment2):
    bounds = jnp.cumsum(counts).astype(jnp.int32)
    slot_index = jnp.arange(SLOTS, dtype=jnp.int32)
    holders = lax.optimization_barrier(jnp.sum((bounds[None, :] <= slot_index[:, None]).astype(jnp.int32), axis=1)).astype(jnp.int32)
    row_index = jnp.arange(ROWS, dtype=jnp.int32)

    def per_slot(totals, inputs):
        hidden_rows, cot_rows, slot_weights, expert, live_count = inputs
        masked = jnp.where((row_index < live_count)[:, None], cot_rows, jnp.zeros_like(cot_rows))
        grads_in = jnp.dot(masked, slot_weights.T, preferred_element_type=jnp.float32).astype(jnp.bfloat16)
        slot_grads = jnp.dot(hidden_rows.T, masked, preferred_element_type=jnp.float32).astype(jnp.bfloat16)
        totals = totals.at[expert].add(slot_grads.astype(jnp.float32))
        return (totals, grads_in)
    empty = jnp.zeros((EXPERTS, HID, D), jnp.float32)
    expert_grads, input_grads = lax.scan(per_slot, empty, (saved, cotangent, weights, holders, live_rows))
    first = BETA_ONE * moment1.astype(jnp.float32) + (1.0 - BETA_ONE) * expert_grads
    second = BETA_TWO * moment2.astype(jnp.float32) + (1.0 - BETA_TWO) * expert_grads * expert_grads
    update = first / BIAS_ONE / (jnp.sqrt(second / BIAS_TWO) + EPSILON) + DECAY_RATE * master
    master_out = master - LEARN_RATE * update
    next_weights = jnp.take(master_out.astype(jnp.bfloat16), next_map, axis=0)
    return (input_grads, master_out, first.astype(jnp.bfloat16), second.astype(jnp.bfloat16), next_weights)
```

```python
import functools
import jax
import jax.numpy as jnp
from jax import lax
from jax.experimental import pallas as pl
from jax.experimental.pallas import tpu as pltpu
from jax.sharding import PartitionSpec as P

LEARN_RATE = 0.001
DECAY_RATE = 0.1
BETA_ONE = 0.9
BETA_TWO = 0.95
BIAS_ONE = 1.0 - 0.9**20
BIAS_TWO = 1.0 - 0.95**20
EPSILON = 1e-08

LANES = 128
GROUP = 4


def contract_cols(left, right):
    return lax.dot_general(
        left, right, (((1,), (1,)), ((), ())), preferred_element_type=jnp.float32
    )


def grads_kernel(live_ref, saved_ref, cot_ref, out_ref, turned, sums, chunk):
    step = pl.program_id(0)
    rows, hidden = saved_ref.shape
    blocks = sums.shape[0]
    wide = cot_ref.shape[1]
    per_step = wide // LANES
    devices = out_ref.shape[0]
    share = hidden // devices

    @pl.when(step == 0)
    def _():
        index = lax.broadcasted_iota(jnp.int32, (rows, hidden), 0)
        kept = jnp.where(index < live_ref[0], saved_ref[...], jnp.zeros_like(saved_ref))
        turned[...] = kept.T

    product = jnp.dot(turned[...], cot_ref[...], preferred_element_type=jnp.float32)
    for part in range(per_step):
        sums[step * per_step + part] = product[:, part * LANES : (part + 1) * LANES]

    @pl.when(step == pl.num_programs(0) - 1)
    def _():
        @pl.loop(0, devices // GROUP)
        def _(group):
            base = pl.multiple_of(group * GROUP * share, 8)
            tall = GROUP * share
            for block in range(blocks):
                piece = sums[block, pl.ds(base, tall), :]
                for member in range(GROUP):
                    chunk[member, block * share : (block + 1) * share, :] = piece[
                        member * share : (member + 1) * share, :
                    ]
            for member in range(GROUP):
                out_ref[group * GROUP + member] = chunk[member].astype(jnp.bfloat16)


def slot_chunks(saved, cot, live, devices):
    rows, hidden = saved.shape
    width = cot.shape[1]
    wide = 2 * LANES
    share = hidden // devices
    blocks = width // LANES
    return pl.pallas_call(
        grads_kernel,
        out_shape=jax.ShapeDtypeStruct((devices, blocks * share, LANES), jnp.bfloat16),
        grid_spec=pltpu.PrefetchScalarGridSpec(
            num_scalar_prefetch=1,
            grid=(width // wide,),
            in_specs=[
                pl.BlockSpec((rows, hidden), lambda n, live: (0, 0), pipeline_mode=pl.Buffered(1)),
                pl.BlockSpec((rows, wide), lambda n, live: (0, n)),
            ],
            out_specs=pl.BlockSpec((devices, blocks * share, LANES), lambda n, live: (0, 0, 0)),
            scratch_shapes=[
                pltpu.VMEM((hidden, rows), jnp.bfloat16),
                pltpu.VMEM((blocks, hidden, LANES), jnp.float32),
                pltpu.VMEM((GROUP, blocks * share, LANES), jnp.float32),
            ],
        ),
        compiler_params=pltpu.CompilerParams(
            dimension_semantics=("arbitrary",), vmem_limit_bytes=40 << 20
        ),
        cost_estimate=pl.CostEstimate(
            flops=2 * rows * hidden * width,
            bytes_accessed=2 * (rows * hidden + rows * width + hidden * width),
            transcendentals=0,
        ),
        name="slot_chunks",
    )(live, saved, cot)


def adam_kernel(
    holder_ref, fresh_ref, next_ref, pieces_ref, master_ref, one_ref, two_ref,
    master_out, one_out, two_out, send_out,
    grads, master_in, one_in, two_in, new_master, new_one, new_two, ready, load_sem, store_sem, send_sem,
):
    slots, height, _ = pieces_ref.shape
    share, experts, width = master_ref.shape
    blocks = width // LANES

    def loads(row):
        return (
            pltpu.make_async_copy(master_ref.at[row], master_in.at[row], load_sem.at[0, row]),
            pltpu.make_async_copy(one_ref.at[row], one_in.at[row], load_sem.at[1, row]),
            pltpu.make_async_copy(two_ref.at[row], two_in.at[row], load_sem.at[2, row]),
        )

    def stores(row):
        return (
            pltpu.make_async_copy(new_master.at[row], master_out.at[row], store_sem.at[0, row]),
            pltpu.make_async_copy(new_one.at[row], one_out.at[row], store_sem.at[1, row]),
            pltpu.make_async_copy(new_two.at[row], two_out.at[row], store_sem.at[2, row]),
        )

    for row in range(share):
        for copy in loads(row):
            copy.start()

    def add_slot(slot, total):
        total = jnp.where(fresh_ref[slot] > 0, 0.0, total) + pieces_ref[slot].astype(jnp.float32)
        grads[pl.ds(holder_ref[slot], height, stride=experts), :] = total
        return total

    lax.fori_loop(0, slots, add_slot, jnp.zeros((height, LANES), jnp.float32), unroll=4)

    for row in range(share):
        for copy in loads(row):
            copy.wait()

        @pl.loop(0, blocks)
        def _(block):
            lanes = pl.ds(pl.multiple_of(block * LANES, LANES), LANES)
            place = pl.ds(pl.multiple_of((block * share + row) * experts, experts), experts)
            grad = grads[place, :]
            old = master_in[row, :, lanes]
            first = BETA_ONE * one_in[row, :, lanes].astype(jnp.float32) + (1.0 - BETA_ONE) * grad
            second = (
                BETA_TWO * two_in[row, :, lanes].astype(jnp.float32)
                + (1.0 - BETA_TWO) * grad * grad
            )
            update = (
                first * (1.0 / BIAS_ONE) / (jnp.sqrt(second * (1.0 / BIAS_TWO)) + EPSILON)
                + DECAY_RATE * old
            )
            new = old - LEARN_RATE * update
            new_master[row, :, lanes] = new
            new_one[row, :, lanes] = first.astype(jnp.bfloat16)
            new_two[row, :, lanes] = second.astype(jnp.bfloat16)
            grads[place, :] = new

        for copy in stores(row):
            copy.start()

    @pl.loop(0, experts)
    def _(expert):
        ready[expert] = grads[pl.ds(expert, height, stride=experts), :].astype(jnp.bfloat16)

    @pl.loop(0, slots)
    def _(slot):
        pltpu.make_async_copy(ready.at[next_ref[slot]], send_out.at[slot], send_sem.at[0]).start()

    for row in range(share):
        for copy in stores(row):
            copy.wait()
    pltpu.make_async_copy(send_out, send_out, send_sem.at[0]).wait()


def adam_step(holder, fresh, next_map, pieces, master, one, two):
    slots, height, _ = pieces.shape
    share, experts, width = master.shape
    space = pl.BlockSpec(memory_space=pl.ANY)
    return pl.pallas_call(
        adam_kernel,
        out_shape=(
            jax.ShapeDtypeStruct(master.shape, jnp.float32),
            jax.ShapeDtypeStruct(one.shape, jnp.bfloat16),
            jax.ShapeDtypeStruct(two.shape, jnp.bfloat16),
            jax.ShapeDtypeStruct((slots, height, LANES), jnp.bfloat16),
        ),
        grid_spec=pltpu.PrefetchScalarGridSpec(
            num_scalar_prefetch=3,
            grid=(1,),
            in_specs=[
                pl.BlockSpec(pieces.shape, lambda i, *s: (0, 0, 0), pipeline_mode=pl.Buffered(1)),
                space, space, space,
            ],
            out_specs=(space, space, space, space),
            scratch_shapes=[
                pltpu.VMEM((height * experts, LANES), jnp.float32),
                pltpu.VMEM(master.shape, jnp.float32),
                pltpu.VMEM(one.shape, jnp.bfloat16),
                pltpu.VMEM(two.shape, jnp.bfloat16),
                pltpu.VMEM(master.shape, jnp.float32),
                pltpu.VMEM(one.shape, jnp.bfloat16),
                pltpu.VMEM(two.shape, jnp.bfloat16),
                pltpu.VMEM((experts, height, LANES), jnp.bfloat16),
                pltpu.SemaphoreType.DMA((3, share)),
                pltpu.SemaphoreType.DMA((3, share)),
                pltpu.SemaphoreType.DMA((1,)),
            ],
        ),
        compiler_params=pltpu.CompilerParams(
            dimension_semantics=("arbitrary",), vmem_limit_bytes=40 << 20
        ),
        name="adam_step",
    )(holder, fresh, next_map, pieces, master, one, two)


def rows_kernel(in_ref, out_ref, chunk, tall):
    groups = in_ref.shape[0] // GROUP
    width = out_ref.shape[1]
    blocks = width // LANES
    share = in_ref.shape[1] // blocks
    height = GROUP * share

    @pl.loop(0, groups)
    def _(group):
        for member in range(GROUP):
            chunk[member] = in_ref[group * GROUP + member].astype(jnp.float32)
        base = pl.multiple_of(group * height, 8)
        for block in range(blocks):
            for member in range(GROUP):
                tall[block, member * share : (member + 1) * share, :] = chunk[
                    member, block * share : (block + 1) * share, :
                ]
            out_ref[pl.ds(base, height), block * LANES : (block + 1) * LANES] = tall[
                block
            ].astype(jnp.bfloat16)


def chunk_rows(arrived, hidden, width, steps=8):
    slots, height, _ = arrived.shape
    blocks = width // LANES
    share = height // blocks
    return pl.pallas_call(
        rows_kernel,
        out_shape=jax.ShapeDtypeStruct((hidden, width), jnp.bfloat16),
        grid=(steps,),
        in_specs=[pl.BlockSpec((slots // steps, height, LANES), lambda i: (i, 0, 0))],
        out_specs=pl.BlockSpec((hidden // steps, width), lambda i: (i, 0)),
        scratch_shapes=[
            pltpu.VMEM((GROUP, height, LANES), jnp.float32),
            pltpu.VMEM((blocks, GROUP * share, LANES), jnp.float32),
        ],
        compiler_params=pltpu.CompilerParams(
            dimension_semantics=("arbitrary",), vmem_limit_bytes=20 << 20
        ),
        name="chunk_rows",
    )(arrived)


def exchange(chunks):
    return lax.all_to_all(chunks, "dev", split_axis=0, concat_axis=0, tiled=True)


def per_device(saved, cotangent, weights, counts, live_rows, next_map, master, moment1, moment2):
    cot_rows = cotangent[0]
    devices = lax.axis_size("dev")
    experts, share, width = master.shape
    hidden = saved.shape[2]
    row_count = saved.shape[1]
    chunks = slot_chunks(saved[0], cot_rows, live_rows, devices)
    received = exchange(chunks)
    row_index = jnp.arange(row_count, dtype=jnp.int32)
    masked = jnp.where(
        (row_index < live_rows[0])[:, None], cot_rows, jnp.zeros_like(cot_rows)
    )
    input_grads = contract_cols(masked, weights[0]).astype(jnp.bfloat16)
    slot_index = jnp.arange(devices, dtype=jnp.int32)
    bounds = jnp.cumsum(counts)
    holders = jnp.sum((bounds[None, :] <= slot_index[:, None]).astype(jnp.int32), axis=1)
    fresh = jnp.any(bounds[None, :] == slot_index[:, None], axis=1) | (slot_index == 0)
    new_master, new_one, new_two, outgoing = adam_step(
        holders, fresh.astype(jnp.int32), next_map, received,
        master.transpose(1, 0, 2), moment1.transpose(1, 0, 2), moment2.transpose(1, 0, 2),
    )
    arriving = exchange(outgoing)
    next_weights = chunk_rows(arriving, hidden, width)
    return (
        input_grads[None],
        new_master.transpose(1, 0, 2),
        new_one.transpose(1, 0, 2),
        new_two.transpose(1, 0, 2),
        next_weights[None],
    )


def solution(mesh):
    placed = (
        P("dev", None, None),
        P("dev", None, None),
        P("dev", None, None),
        P(),
        P("dev"),
        P(),
        P(None, "dev", None),
        P(None, "dev", None),
        P(None, "dev", None),
    )
    return jax.shard_map(
        per_device,
        mesh=mesh,
        in_specs=placed,
        out_specs=(
            P("dev", None, None),
            P(None, "dev", None),
            P(None, "dev", None),
            P(None, "dev", None),
            P("dev", None, None),
        ),
        check_vma=False,
    )
```

```python
import functools
import jax
import jax.numpy as jnp
from jax import lax
from jax.experimental import pallas as pl
from jax.experimental.pallas import tpu as pltpu
from jax.sharding import PartitionSpec as P

LEARN_RATE = 0.001
DECAY_RATE = 0.1
BETA_ONE = 0.9
BETA_TWO = 0.95
BIAS_ONE = 1.0 - 0.9**20
BIAS_TWO = 1.0 - 0.95**20
EPSILON = 1e-08

LANES = 128
GROUP = 4


def contract_cols(left, right):
    return lax.dot_general(
        left, right, (((1,), (1,)), ((), ())), preferred_element_type=jnp.float32
    )


FAR = pl.BlockSpec(memory_space=pltpu.HBM)
NEAR = pl.BlockSpec(memory_space=pltpu.VMEM)
SCALARS = pl.BlockSpec(memory_space=pltpu.SMEM)


def grads_kernel(
    live_ref, saved_ref, cot_ref, out_ref,
    saved_in, cot_in, turned, sums, chunk, packed, saved_sem, cot_sem, out_sem,
):
    rows, hidden = saved_ref.shape
    steps, _, wide = cot_in.shape
    blocks = sums.shape[0]
    per_step = wide // LANES
    devices = out_ref.shape[0]
    share = hidden // devices
    tall = GROUP * share
    parts = out_sem.shape[0]
    part_size = devices // parts
    bands = saved_sem.shape[0]
    band_rows = rows // bands

    def load_saved(band):
        span = pl.ds(band * band_rows, band_rows)
        return pltpu.make_async_copy(saved_ref.at[span], saved_in.at[span], saved_sem.at[band])

    def load_cot(step):
        return pltpu.make_async_copy(
            cot_ref.at[:, step * wide : (step + 1) * wide], cot_in.at[step], cot_sem.at[step]
        )

    def send(part):
        span = pl.ds(part * part_size, part_size)
        return pltpu.make_async_copy(packed.at[span], out_ref.at[span], out_sem.at[part])

    for band in range(bands):
        load_saved(band).start()

    @pl.loop(0, bands)
    def _(band):
        span = pl.ds(pl.multiple_of(band * band_rows, band_rows), band_rows)
        pltpu.make_async_copy(saved_ref.at[span], saved_in.at[span], saved_sem.at[band]).wait()

        @pl.when(band == 0)
        def _():
            for step in range(steps):
                load_cot(step).start()

        index = lax.broadcasted_iota(jnp.int32, (band_rows, hidden), 0)
        part = saved_in[span, :]
        turned[:, span] = jnp.where(
            index < live_ref[0] - band * band_rows, part, jnp.zeros_like(part)
        ).T

    @pl.loop(0, steps)
    def _(step):
        pltpu.make_async_copy(cot_ref.at[:, :wide], cot_in.at[step], cot_sem.at[step]).wait()
        for start in range(0, wide, 2 * LANES):
            product = jnp.dot(
                turned[...],
                cot_in[step, :, start : start + 2 * LANES],
                preferred_element_type=jnp.float32,
            )
            for part in range(2):
                sums[step * per_step + start // LANES + part] = product[
                    :, part * LANES : (part + 1) * LANES
                ]

    for part in range(parts):

        @pl.loop(part * part_size // GROUP, (part + 1) * part_size // GROUP)
        def _(group):
            base = pl.multiple_of(group * tall, 8)
            for block in range(blocks):
                piece = sums[block, pl.ds(base, tall), :]
                for member in range(GROUP):
                    chunk[member, block * share : (block + 1) * share, :] = piece[
                        member * share : (member + 1) * share, :
                    ]
            for member in range(GROUP):
                packed[group * GROUP + member] = chunk[member].astype(jnp.bfloat16)

        send(part).start()
    for part in range(parts):
        send(part).wait()


def slot_chunks(saved, cot, live, devices, steps=4, parts=4, bands=4):
    rows, hidden = saved.shape
    width = cot.shape[1]
    wide = width // steps
    share = hidden // devices
    blocks = width // LANES
    return pl.pallas_call(
        grads_kernel,
        out_shape=jax.ShapeDtypeStruct((devices, blocks * share, LANES), jnp.bfloat16),
        in_specs=[SCALARS, FAR, FAR],
        out_specs=FAR,
        scratch_shapes=[
            pltpu.VMEM((rows, hidden), jnp.bfloat16),
            pltpu.VMEM((steps, rows, wide), jnp.bfloat16),
            pltpu.VMEM((hidden, rows), jnp.bfloat16),
            pltpu.VMEM((blocks, hidden, LANES), jnp.float32),
            pltpu.VMEM((GROUP, blocks * share, LANES), jnp.float32),
            pltpu.VMEM((devices, blocks * share, LANES), jnp.bfloat16),
            pltpu.SemaphoreType.DMA((bands,)),
            pltpu.SemaphoreType.DMA((steps,)),
            pltpu.SemaphoreType.DMA((parts,)),
        ],
        compiler_params=pltpu.CompilerParams(vmem_limit_bytes=63 << 20),
        cost_estimate=pl.CostEstimate(
            flops=2 * rows * hidden * width,
            bytes_accessed=2 * (rows * hidden + rows * width + hidden * width),
            transcendentals=0,
        ),
        name="slot_chunks",
    )(live, saved, cot)


def adam_kernel(
    holder_ref, fresh_ref, next_ref, pieces, master_ref, one_ref, two_ref,
    master_out, one_out, two_out, send_out,
    sums, master, one, two, outgoing, load_sem, store_sem, send_sem,
):
    slots, height, _ = pieces.shape
    share, experts, width = master_ref.shape
    blocks = width // LANES
    deep = 16
    tiles = experts // deep
    quad = GROUP * share
    arrays = ((master_ref, master, master_out), (one_ref, one, one_out), (two_ref, two, two_out))
    sends = send_sem.shape[0]
    send_size = slots // sends

    def loads(tile):
        span = pl.ds(pl.multiple_of(tile * deep, deep), deep)
        return [
            pltpu.make_async_copy(far.at[:, span, :], near.at[:, span, :], load_sem.at[which, tile])
            for which, (far, near, _) in enumerate(arrays)
        ]

    def stores(tile):
        span = pl.ds(pl.multiple_of(tile * deep, deep), deep)
        return [
            pltpu.make_async_copy(near.at[:, span, :], far.at[:, span, :], store_sem.at[which, tile])
            for which, (_, near, far) in enumerate(arrays)
        ]

    def send(part):
        span = pl.ds(part * send_size, send_size)
        return pltpu.make_async_copy(outgoing.at[span], send_out.at[span], send_sem.at[part])

    for tile in range(tiles):
        for copy in loads(tile):
            copy.start()

    def add_slot(slot, total):
        total = jnp.where(fresh_ref[slot] > 0, 0.0, total) + pieces[slot].astype(jnp.float32)
        sums[holder_ref[slot]] = total
        return total

    lax.fori_loop(0, slots, add_slot, jnp.zeros((height, LANES), jnp.float32), unroll=4)

    @pl.loop(0, tiles)
    def _(tile):
        for copy in loads(tile):
            copy.wait()
        rows = pl.ds(pl.multiple_of(tile * deep, deep), deep)

        @pl.loop(0, blocks // GROUP)
        def _(four):
            def place(half, band):
                return (
                    pl.ds(tile * deep + half * 8, 8),
                    pl.ds(pl.multiple_of(four * quad + band * 8, 8), 8),
                )

            for band in range(quad // 8):
                turned = [jnp.swapaxes(sums[place(half, band)], 0, 1) for half in range(2)]
                fresh = ([], [])
                for k in range(8):
                    block, row = divmod(band * 8 + k, share)
                    grad = jnp.concatenate([turned[0][k], turned[1][k]], axis=0)
                    lanes = pl.ds(pl.multiple_of((four * GROUP + block) * LANES, LANES), LANES)
                    first = (
                        BETA_ONE * one[row, rows, lanes].astype(jnp.float32)
                        + (1.0 - BETA_ONE) * grad
                    )
                    second = (
                        BETA_TWO * two[row, rows, lanes].astype(jnp.float32)
                        + (1.0 - BETA_TWO) * (grad * grad)
                    )
                    root = second * lax.rsqrt(second) * BIAS_TWO**-0.5 + EPSILON
                    new = (1.0 - LEARN_RATE * DECAY_RATE) * master[row, rows, lanes] - (
                        (LEARN_RATE / BIAS_ONE) * first
                    ) / root
                    master[row, rows, lanes] = new
                    one[row, rows, lanes] = first.astype(jnp.bfloat16)
                    two[row, rows, lanes] = second.astype(jnp.bfloat16)
                    fresh[0].append(new[:8])
                    fresh[1].append(new[8:])
                for half in range(2):
                    sums[place(half, band)] = jnp.swapaxes(jnp.stack(fresh[half]), 0, 1)

        for copy in stores(tile):
            copy.start()

    for part in range(sends):

        def fill(slot, carry):
            outgoing[slot] = sums[next_ref[slot]].astype(jnp.bfloat16)
            return carry

        lax.fori_loop(part * send_size, (part + 1) * send_size, fill, 0, unroll=4)
        send(part).start()

    for tile in range(tiles):
        for copy in stores(tile):
            copy.wait()
    for part in range(sends):
        send(part).wait()


def adam_step(holder, fresh, next_map, pieces, master, one, two, sends=4):
    slots, height, _ = pieces.shape
    share, experts, width = master.shape
    tiles = experts // 16
    return pl.pallas_call(
        adam_kernel,
        out_shape=(
            pltpu.HBM(master.shape, jnp.float32),
            pltpu.HBM(one.shape, jnp.bfloat16),
            pltpu.HBM(two.shape, jnp.bfloat16),
            pltpu.HBM((slots, height, LANES), jnp.bfloat16),
        ),
        in_specs=[SCALARS] * 3 + [NEAR] + [FAR] * 3,
        out_specs=(FAR,) * 4,
        scratch_shapes=[
            pltpu.VMEM((experts, height, LANES), jnp.float32),
            pltpu.VMEM(master.shape, jnp.float32),
            pltpu.VMEM(one.shape, jnp.bfloat16),
            pltpu.VMEM(two.shape, jnp.bfloat16),
            pltpu.VMEM(pieces.shape, jnp.bfloat16),
            pltpu.SemaphoreType.DMA((3, tiles)),
            pltpu.SemaphoreType.DMA((3, tiles)),
            pltpu.SemaphoreType.DMA((sends,)),
        ],
        compiler_params=pltpu.CompilerParams(vmem_limit_bytes=60 << 20),
        name="adam_step",
    )(
        holder, fresh, next_map, pltpu.with_memory_space_constraint(pieces, pltpu.VMEM),
        master, one, two,
    )


def rows_kernel(arrived, out_ref, wholes, chunk, tall, out_sem):
    slots, depth, _ = arrived.shape
    width = out_ref.shape[1]
    members = chunk.shape[0]
    blocks = width // LANES
    share = depth // blocks
    height = members * share
    parts = out_sem.shape[0]
    part_size = slots // parts

    def store(part):
        span = pl.ds(part * part_size * share, part_size * share)
        return pltpu.make_async_copy(wholes.at[span], out_ref.at[span], out_sem.at[part])

    for part in range(parts):

        @pl.loop(part * part_size // members, (part + 1) * part_size // members)
        def _(group):
            for member in range(members):
                chunk[member] = arrived[group * members + member].astype(jnp.float32)
            base = pl.multiple_of(group * height, 16)
            for block in range(blocks):
                for member in range(members):
                    tall[block, member * share : (member + 1) * share, :] = chunk[
                        member, block * share : (block + 1) * share, :
                    ]
                wholes[pl.ds(base, height), block * LANES : (block + 1) * LANES] = tall[
                    block
                ].astype(jnp.bfloat16)

        store(part).start()
    for part in range(parts):
        store(part).wait()


def chunk_rows(arrived, hidden, width, parts=4, members=8):
    slots, height, _ = arrived.shape
    blocks = width // LANES
    share = height // blocks
    return pl.pallas_call(
        rows_kernel,
        out_shape=jax.ShapeDtypeStruct((hidden, width), jnp.bfloat16),
        in_specs=[NEAR],
        out_specs=FAR,
        scratch_shapes=[
            pltpu.VMEM((hidden, width), jnp.bfloat16),
            pltpu.VMEM((members, height, LANES), jnp.float32),
            pltpu.VMEM((blocks, members * share, LANES), jnp.float32),
            pltpu.SemaphoreType.DMA((parts,)),
        ],
        compiler_params=pltpu.CompilerParams(vmem_limit_bytes=32 << 20),
        name="chunk_rows",
    )(pltpu.with_memory_space_constraint(arrived, pltpu.VMEM))


def exchange(chunks):
    return lax.all_to_all(chunks, "dev", split_axis=0, concat_axis=0, tiled=True)


def per_device(saved, cotangent, weights, counts, live_rows, next_map, master, moment1, moment2):
    cot_rows = cotangent[0]
    devices = lax.axis_size("dev")
    experts, share, width = master.shape
    hidden = saved.shape[2]
    row_count = saved.shape[1]
    chunks = slot_chunks(saved[0], cot_rows, live_rows, devices)
    received = exchange(chunks)
    row_index = jnp.arange(row_count, dtype=jnp.int32)
    masked = jnp.where(
        (row_index < live_rows[0])[:, None], cot_rows, jnp.zeros_like(cot_rows)
    )
    input_grads = contract_cols(masked, weights[0]).astype(jnp.bfloat16)
    slot_index = jnp.arange(devices, dtype=jnp.int32)
    bounds = jnp.cumsum(counts)
    holders = jnp.sum((bounds[None, :] <= slot_index[:, None]).astype(jnp.int32), axis=1)
    fresh = jnp.any(bounds[None, :] == slot_index[:, None], axis=1) | (slot_index == 0)
    new_master, new_one, new_two, outgoing = adam_step(
        holders, fresh.astype(jnp.int32), next_map, received,
        master.transpose(1, 0, 2), moment1.transpose(1, 0, 2), moment2.transpose(1, 0, 2),
    )
    arriving = exchange(outgoing)
    next_weights = chunk_rows(arriving, hidden, width)
    return (
        input_grads[None],
        new_master.transpose(1, 0, 2),
        new_one.transpose(1, 0, 2),
        new_two.transpose(1, 0, 2),
        next_weights[None],
    )


def solution(mesh):
    placed = (
        P("dev", None, None),
        P("dev", None, None),
        P("dev", None, None),
        P(),
        P("dev"),
        P(),
        P(None, "dev", None),
        P(None, "dev", None),
        P(None, "dev", None),
    )
    return jax.shard_map(
        per_device,
        mesh=mesh,
        in_specs=placed,
        out_specs=(
            P("dev", None, None),
            P(None, "dev", None),
            P(None, "dev", None),
            P(None, "dev", None),
            P("dev", None, None),
        ),
        check_vma=False,
    )
```

```python
import functools
import jax
import jax.numpy as jnp
from jax import lax
from jax.experimental import pallas as pl
from jax.experimental.pallas import tpu as pltpu
from jax.sharding import PartitionSpec as P

LEARN_RATE = 0.001
DECAY_RATE = 0.1
BETA_ONE = 0.9
BETA_TWO = 0.95
BIAS_ONE = 1.0 - 0.9**20
BIAS_TWO = 1.0 - 0.95**20
EPSILON = 1e-08

LANES = 128
GROUP = 4


def contract_cols(left, right):
    return lax.dot_general(
        left, right, (((1,), (1,)), ((), ())), preferred_element_type=jnp.float32
    )


FAR = pl.BlockSpec(memory_space=pltpu.HBM)
NEAR = pl.BlockSpec(memory_space=pltpu.VMEM)
SCALARS = pl.BlockSpec(memory_space=pltpu.SMEM)


def grads_kernel(
    live_ref, saved_ref, cot_ref, out_ref,
    live, saved_in, cot_in, turned, spread, packed, live_sem, saved_sem, cot_sem, out_sem,
):
    rows, hidden = saved_ref.shape
    steps, _, wide = cot_in.shape
    devices = out_ref.shape[0]
    share = hidden // devices
    parts = out_sem.shape[0]
    part_size = devices // parts
    bands = saved_sem.shape[0]
    band_rows = rows // bands

    def load_saved(band):
        span = pl.ds(band * band_rows, band_rows)
        return pltpu.make_async_copy(saved_ref.at[span], saved_in.at[span], saved_sem.at[band])

    def load_cot(step):
        return pltpu.make_async_copy(
            cot_ref.at[:, step * wide : (step + 1) * wide], cot_in.at[step], cot_sem.at[step]
        )

    def send(part):
        span = pl.ds(part * part_size, part_size)
        return pltpu.make_async_copy(packed.at[span], out_ref.at[span], out_sem.at[part])

    load_live = pltpu.make_async_copy(live_ref, live, live_sem.at[0])
    load_live.start()
    for band in range(bands):
        load_saved(band).start()
    load_live.wait()

    @pl.loop(0, bands)
    def _(band):
        span = pl.ds(pl.multiple_of(band * band_rows, band_rows), band_rows)
        pltpu.make_async_copy(saved_ref.at[span], saved_in.at[span], saved_sem.at[band]).wait()

        @pl.when(band == 0)
        def _():
            load_cot(0).start()

        index = lax.broadcasted_iota(jnp.int32, (band_rows, hidden), 0)
        part = saved_in[span, :]
        turned[:, span] = jnp.where(
            index < live[0] - band * band_rows, part, jnp.zeros_like(part)
        ).T

    load_cot(1).start()

    @pl.loop(0, steps)
    def _(step):
        pltpu.make_async_copy(cot_ref.at[:, :wide], cot_in.at[step], cot_sem.at[step]).wait()

        @pl.when(step + 2 < steps)
        def _():
            later = step + 2
            span = pl.ds(pl.multiple_of(later * wide, wide), wide)
            pltpu.make_async_copy(
                cot_ref.at[:, span], cot_in.at[later], cot_sem.at[later]
            ).start()

        for start in range(0, wide, 2 * LANES):
            product = jnp.dot(
                turned[...],
                cot_in[step, :, start : start + 2 * LANES],
                preferred_element_type=jnp.float32,
            )
            for part in range(2):
                block = start // LANES + part
                for device in range(devices):
                    spread[step, device, block * share : (block + 1) * share, :] = product[
                        device * share : (device + 1) * share, part * LANES : (part + 1) * LANES
                    ]

    for part in range(parts):

        @pl.loop(part * part_size // GROUP, (part + 1) * part_size // GROUP)
        def _(group):
            for member in range(GROUP):
                device = group * GROUP + member
                packed[device] = jnp.concatenate(
                    [spread[step, device] for step in range(steps)], axis=0
                ).astype(jnp.bfloat16)

        send(part).start()
    for part in range(parts):
        send(part).wait()


def slot_chunks(saved, cot, live, devices, steps=4, parts=4, bands=4):
    rows, hidden = saved.shape
    width = cot.shape[1]
    wide = width // steps
    share = hidden // devices
    blocks = width // LANES
    return pl.pallas_call(
        grads_kernel,
        out_shape=jax.ShapeDtypeStruct((devices, blocks * share, LANES), jnp.bfloat16),
        in_specs=[FAR, FAR, FAR],
        out_specs=FAR,
        scratch_shapes=[
            pltpu.SMEM((1,), jnp.int32),
            pltpu.VMEM((rows, hidden), jnp.bfloat16),
            pltpu.VMEM((steps, rows, wide), jnp.bfloat16),
            pltpu.VMEM((hidden, rows), jnp.bfloat16),
            pltpu.VMEM((steps, devices, wide // LANES * share, LANES), jnp.float32),
            pltpu.VMEM((devices, blocks * share, LANES), jnp.bfloat16),
            pltpu.SemaphoreType.DMA((1,)),
            pltpu.SemaphoreType.DMA((bands,)),
            pltpu.SemaphoreType.DMA((steps,)),
            pltpu.SemaphoreType.DMA((parts,)),
        ],
        compiler_params=pltpu.CompilerParams(vmem_limit_bytes=63 << 20),
        cost_estimate=pl.CostEstimate(
            flops=2 * rows * hidden * width,
            bytes_accessed=2 * (rows * hidden + rows * width + hidden * width),
            transcendentals=0,
        ),
        name="slot_chunks",
    )(live, saved, cot)


def adam_kernel(
    holder_ref, fresh_ref, next_ref, pieces, master_ref, one_ref, two_ref,
    master_out, one_out, two_out, send_out,
    sums, master, one, two, outgoing, load_sem, store_sem, send_sem,
):
    slots, height, _ = pieces.shape
    share, experts, width = master_ref.shape
    blocks = width // LANES
    deep = 16
    tiles = experts // deep
    quad = GROUP * share
    pitch = sums.shape[0] // experts
    arrays = ((master_ref, master, master_out), (one_ref, one, one_out), (two_ref, two, two_out))
    sends = send_sem.shape[0]
    send_size = slots // sends

    def loads(tile):
        span = pl.ds(pl.multiple_of(tile * deep, deep), deep)
        return [
            pltpu.make_async_copy(far.at[:, span, :], near.at[:, span, :], load_sem.at[which, tile])
            for which, (far, near, _) in enumerate(arrays)
        ]

    def stores(tile):
        span = pl.ds(pl.multiple_of(tile * deep, deep), deep)
        return [
            pltpu.make_async_copy(near.at[:, span, :], far.at[:, span, :], store_sem.at[which, tile])
            for which, (_, near, far) in enumerate(arrays)
        ]

    def send(part):
        span = pl.ds(part * send_size, send_size)
        return pltpu.make_async_copy(outgoing.at[span], send_out.at[span], send_sem.at[part])

    for tile in range(tiles):
        for copy in loads(tile):
            copy.start()

    def add_slot(slot, total):
        total = jnp.where(fresh_ref[slot] > 0, 0.0, total) + pieces[slot].astype(jnp.float32)
        sums[pl.ds(holder_ref[slot] * pitch, height), :] = total
        return total

    lax.fori_loop(0, slots, add_slot, jnp.zeros((height, LANES), jnp.float32), unroll=4)

    @pl.loop(0, tiles)
    def _(tile):
        for copy in loads(tile):
            copy.wait()
        rows = pl.ds(pl.multiple_of(tile * deep, deep), deep)

        @pl.loop(0, blocks // GROUP)
        def _(four):
            for k in range(quad):
                block, row = divmod(k, share)
                place = pl.ds(tile * (deep * pitch) + four * quad + k, deep, stride=pitch)
                lanes = pl.ds(pl.multiple_of((four * GROUP + block) * LANES, LANES), LANES)
                grad = sums[place, :]
                first = (
                    BETA_ONE * one[row, rows, lanes].astype(jnp.float32)
                    + (1.0 - BETA_ONE) * grad
                )
                second = (
                    BETA_TWO * two[row, rows, lanes].astype(jnp.float32)
                    + (1.0 - BETA_TWO) * (grad * grad)
                )
                root = second * lax.rsqrt(second) + EPSILON * BIAS_TWO**0.5
                new = (1.0 - LEARN_RATE * DECAY_RATE) * master[row, rows, lanes] - (
                    (LEARN_RATE / BIAS_ONE * BIAS_TWO**0.5) * first
                ) / root
                master[row, rows, lanes] = new
                one[row, rows, lanes] = first.astype(jnp.bfloat16)
                two[row, rows, lanes] = second.astype(jnp.bfloat16)
                sums[place, :] = new

        for copy in stores(tile):
            copy.start()

    for part in range(sends):

        def fill(slot, carry):
            outgoing[slot] = sums[pl.ds(next_ref[slot] * pitch, height), :].astype(jnp.bfloat16)
            return carry

        lax.fori_loop(part * send_size, (part + 1) * send_size, fill, 0, unroll=4)
        send(part).start()

    for tile in range(tiles):
        for copy in stores(tile):
            copy.wait()
    for part in range(sends):
        send(part).wait()


def adam_step(holder, fresh, next_map, pieces, master, one, two, sends=4):
    slots, height, _ = pieces.shape
    share, experts, width = master.shape
    tiles = experts // 16
    return pl.pallas_call(
        adam_kernel,
        out_shape=(
            pltpu.HBM(master.shape, jnp.float32),
            pltpu.HBM(one.shape, jnp.bfloat16),
            pltpu.HBM(two.shape, jnp.bfloat16),
            pltpu.HBM((slots, height, LANES), jnp.bfloat16),
        ),
        in_specs=[SCALARS] * 3 + [NEAR] + [FAR] * 3,
        out_specs=(FAR,) * 4,
        scratch_shapes=[
            pltpu.VMEM((experts * (height + 1), LANES), jnp.float32),
            pltpu.VMEM(master.shape, jnp.float32),
            pltpu.VMEM(one.shape, jnp.bfloat16),
            pltpu.VMEM(two.shape, jnp.bfloat16),
            pltpu.VMEM(pieces.shape, jnp.bfloat16),
            pltpu.SemaphoreType.DMA((3, tiles)),
            pltpu.SemaphoreType.DMA((3, tiles)),
            pltpu.SemaphoreType.DMA((sends,)),
        ],
        compiler_params=pltpu.CompilerParams(vmem_limit_bytes=60 << 20),
        name="adam_step",
    )(
        holder, fresh, next_map, pltpu.with_memory_space_constraint(pieces, pltpu.VMEM),
        master, one, two,
    )


def rows_kernel(arrived, out_ref, wholes, tall, out_sem):
    slots, depth, _ = arrived.shape
    width = out_ref.shape[1]
    blocks = width // LANES
    share = depth // blocks
    height = tall.shape[1]
    members = height // share
    parts = out_sem.shape[0]
    part_size = slots // parts

    def store(part):
        span = pl.ds(part * part_size * share, part_size * share)
        return pltpu.make_async_copy(wholes.at[span], out_ref.at[span], out_sem.at[part])

    for part in range(parts):

        @pl.loop(part * part_size // members, (part + 1) * part_size // members)
        def _(group):
            base = pl.multiple_of(group * height, 16)
            for member in range(members):
                chunk = arrived[group * members + member].astype(jnp.float32)
                for block in range(blocks):
                    tall[block, member * share : (member + 1) * share, :] = chunk[
                        block * share : (block + 1) * share, :
                    ]
            for block in range(blocks):
                wholes[pl.ds(base, height), block * LANES : (block + 1) * LANES] = tall[
                    block
                ].astype(jnp.bfloat16)

        store(part).start()
    for part in range(parts):
        store(part).wait()


def chunk_rows(arrived, hidden, width, parts=4, members=8):
    slots, height, _ = arrived.shape
    blocks = width // LANES
    share = height // blocks
    return pl.pallas_call(
        rows_kernel,
        out_shape=jax.ShapeDtypeStruct((hidden, width), jnp.bfloat16),
        in_specs=[NEAR],
        out_specs=FAR,
        scratch_shapes=[
            pltpu.VMEM((hidden, width), jnp.bfloat16),
            pltpu.VMEM((blocks, members * share, LANES), jnp.float32),
            pltpu.SemaphoreType.DMA((parts,)),
        ],
        compiler_params=pltpu.CompilerParams(vmem_limit_bytes=32 << 20),
        name="chunk_rows",
    )(pltpu.with_memory_space_constraint(arrived, pltpu.VMEM))


def exchange(chunks):
    return lax.all_to_all(chunks, "dev", split_axis=0, concat_axis=0, tiled=True)


def per_device(saved, cotangent, weights, counts, live_rows, next_map, master, moment1, moment2):
    cot_rows = cotangent[0]
    devices = lax.axis_size("dev")
    experts, share, width = master.shape
    hidden = saved.shape[2]
    row_count = saved.shape[1]
    chunks = slot_chunks(saved[0], cot_rows, live_rows, devices)
    received = exchange(chunks)
    row_index = jnp.arange(row_count, dtype=jnp.int32)
    masked = jnp.where(
        (row_index < live_rows[0])[:, None], cot_rows, jnp.zeros_like(cot_rows)
    )
    input_grads = contract_cols(masked, weights[0]).astype(jnp.bfloat16)
    slot_index = jnp.arange(devices, dtype=jnp.int32)
    bounds = jnp.cumsum(counts)
    holders = jnp.sum((bounds[None, :] <= slot_index[:, None]).astype(jnp.int32), axis=1)
    fresh = jnp.any(bounds[None, :] == slot_index[:, None], axis=1) | (slot_index == 0)
    new_master, new_one, new_two, outgoing = adam_step(
        holders, fresh.astype(jnp.int32), next_map, received,
        master.transpose(1, 0, 2), moment1.transpose(1, 0, 2), moment2.transpose(1, 0, 2),
    )
    arriving = exchange(outgoing)
    next_weights = chunk_rows(arriving, hidden, width)
    return (
        input_grads[None],
        new_master.transpose(1, 0, 2),
        new_one.transpose(1, 0, 2),
        new_two.transpose(1, 0, 2),
        next_weights[None],
    )


def solution(mesh):
    placed = (
        P("dev", None, None),
        P("dev", None, None),
        P("dev", None, None),
        P(),
        P("dev"),
        P(),
        P(None, "dev", None),
        P(None, "dev", None),
        P(None, "dev", None),
    )
    return jax.shard_map(
        per_device,
        mesh=mesh,
        in_specs=placed,
        out_specs=(
            P("dev", None, None),
            P(None, "dev", None),
            P(None, "dev", None),
            P(None, "dev", None),
            P("dev", None, None),
        ),
        check_vma=False,
    )
```

```python
import functools
import jax
import jax.numpy as jnp
from jax import lax
from jax.experimental import pallas as pl
from jax.experimental.pallas import tpu as pltpu
from jax.sharding import PartitionSpec as P

LEARN_RATE = 0.001
DECAY_RATE = 0.1
BETA_ONE = 0.9
BETA_TWO = 0.95
BIAS_ONE = 1.0 - 0.9**20
BIAS_TWO = 1.0 - 0.95**20
EPSILON = 1e-08

LANES = 128
GROUP = 4


def contract_cols(left, right):
    return lax.dot_general(
        left, right, (((1,), (1,)), ((), ())), preferred_element_type=jnp.float32
    )


FAR = pl.BlockSpec(memory_space=pltpu.HBM)
NEAR = pl.BlockSpec(memory_space=pltpu.VMEM)
SCALARS = pl.BlockSpec(memory_space=pltpu.SMEM)


def grads_kernel(
    live_ref, saved_ref, cot_ref, out_ref,
    saved_in, cot_in, turned, ordered, packed, saved_sem, cot_sem, out_sem,
):
    rows, hidden = saved_ref.shape
    strips, _, thin = cot_in.shape
    steps = packed.shape[0]
    per_step = strips // steps
    devices = out_ref.shape[0]
    share = hidden // devices
    tall = ordered.shape[1]
    bands = saved_sem.shape[0]
    band_rows = rows // bands

    def load_saved(band):
        span = pl.ds(band * band_rows, band_rows)
        return pltpu.make_async_copy(saved_ref.at[span], saved_in.at[span], saved_sem.at[band])

    def load_cot(strip):
        span = pl.ds(strip * thin, thin)
        return pltpu.make_async_copy(cot_ref.at[:, span], cot_in.at[strip], cot_sem.at[strip])

    def send(step):
        span = pl.ds(pl.multiple_of(step * tall, tall), tall)
        return pltpu.make_async_copy(packed.at[step], out_ref.at[:, span], out_sem.at[step])

    def multiply(step, target):
        for which in range(per_step):
            strip = step * per_step + which
            pltpu.make_async_copy(
                cot_ref.at[:, :thin], cot_in.at[strip], cot_sem.at[strip]
            ).wait()
        for which in range(per_step):
            product = jnp.dot(
                turned[...], cot_in[step * per_step + which], preferred_element_type=jnp.float32
            )
            for part in range(thin // LANES):
                block = which * (thin // LANES) + part
                for device in range(devices):
                    target[device, block * share : (block + 1) * share, :] = product[
                        device * share : (device + 1) * share, part * LANES : (part + 1) * LANES
                    ]

    for band in range(bands):
        load_saved(band).start()

    @pl.loop(0, bands)
    def _(band):
        span = pl.ds(pl.multiple_of(band * band_rows, band_rows), band_rows)
        pltpu.make_async_copy(saved_ref.at[span], saved_in.at[span], saved_sem.at[band]).wait()

        @pl.when(band == 0)
        def _():
            for strip in range(per_step):
                load_cot(strip).start()

        index = lax.broadcasted_iota(jnp.int32, (band_rows, hidden), 0)
        part = saved_in[span, :]
        turned[:, span] = jnp.where(
            index < live_ref[0] - band * band_rows, part, jnp.zeros_like(part)
        ).T

    for strip in range(per_step, strips):
        load_cot(strip).start()

    @pl.loop(0, steps)
    def _(step):
        multiply(step, ordered)

        @pl.loop(0, devices // 8)
        def _(eight):
            for member in range(8):
                packed[step, eight * 8 + member] = ordered[eight * 8 + member].astype(jnp.bfloat16)

        send(step).start()

    for step in range(steps):
        send(step).wait()


def slot_chunks(saved, cot, live, devices, steps=4, bands=4):
    rows, hidden = saved.shape
    width = cot.shape[1]
    thin = 2 * LANES
    strips = width // thin
    share = hidden // devices
    blocks = width // LANES
    tall = blocks // steps * share
    return pl.pallas_call(
        grads_kernel,
        out_shape=jax.ShapeDtypeStruct((devices, blocks * share, LANES), jnp.bfloat16),
        in_specs=[SCALARS, FAR, FAR],
        out_specs=FAR,
        scratch_shapes=[
            pltpu.VMEM((rows, hidden), jnp.bfloat16),
            pltpu.VMEM((strips, rows, thin), jnp.bfloat16),
            pltpu.VMEM((hidden, rows), jnp.bfloat16),
            pltpu.VMEM((devices, tall, LANES), jnp.float32),
            pltpu.VMEM((steps, devices, tall, LANES), jnp.bfloat16),
            pltpu.SemaphoreType.DMA((bands,)),
            pltpu.SemaphoreType.DMA((strips,)),
            pltpu.SemaphoreType.DMA((steps,)),
        ],
        compiler_params=pltpu.CompilerParams(vmem_limit_bytes=63 << 20),
        cost_estimate=pl.CostEstimate(
            flops=2 * rows * hidden * width,
            bytes_accessed=2 * (rows * hidden + rows * width + hidden * width),
            transcendentals=0,
        ),
        name="slot_chunks",
    )(live, saved, cot)


def inputs_kernel(live_ref, cot_ref, weights_ref, out_ref):
    tall = cot_ref.shape[0]
    index = lax.broadcasted_iota(jnp.int32, out_ref.shape, 0) + pl.program_id(0) * tall
    product = contract_cols(cot_ref[...], weights_ref[...])
    out_ref[...] = jnp.where(index < live_ref[0], product, 0.0).astype(jnp.bfloat16)


def input_rows(cot, weights, live, steps=4):
    rows, width = cot.shape
    hidden = weights.shape[0]
    return pl.pallas_call(
        inputs_kernel,
        out_shape=jax.ShapeDtypeStruct((rows, hidden), jnp.bfloat16),
        grid=(steps,),
        in_specs=[
            SCALARS,
            pl.BlockSpec((rows // steps, width), lambda i: (i, 0)),
            pl.BlockSpec((hidden, width), lambda i: (0, 0)),
        ],
        out_specs=pl.BlockSpec((rows // steps, hidden), lambda i: (i, 0)),
        compiler_params=pltpu.CompilerParams(
            dimension_semantics=("arbitrary",), vmem_limit_bytes=40 << 20
        ),
        cost_estimate=pl.CostEstimate(
            flops=2 * rows * hidden * width,
            bytes_accessed=2 * (rows * hidden + rows * width + hidden * width),
            transcendentals=0,
        ),
        name="input_rows",
    )(live, cot, weights)


def adam_kernel(
    holder_far, fresh_far, next_far, pieces, master_ref, one_ref, two_ref,
    master_out, one_out, two_out, send_out,
    holder_ref, fresh_ref, next_ref, sums, master, one, two, outgoing,
    table_sem, load_sem, store_sem, send_sem,
):
    slots, height, _ = pieces.shape
    share, experts, width = master_ref.shape
    blocks = width // LANES
    deep = 16
    tiles = experts // deep
    quad = GROUP * share
    pitch = sums.shape[0] // experts
    arrays = ((master_ref, master, master_out), (one_ref, one, one_out), (two_ref, two, two_out))
    sends = send_sem.shape[0]
    send_size = slots // sends

    def loads(tile):
        span = pl.ds(pl.multiple_of(tile * deep, deep), deep)
        return [
            pltpu.make_async_copy(far.at[:, span, :], near.at[:, span, :], load_sem.at[which, tile])
            for which, (far, near, _) in enumerate(arrays)
        ]

    def stores(tile):
        span = pl.ds(pl.multiple_of(tile * deep, deep), deep)
        return [
            pltpu.make_async_copy(near.at[:, span, :], far.at[:, span, :], store_sem.at[which, tile])
            for which, (_, near, far) in enumerate(arrays)
        ]

    def send(part):
        span = pl.ds(part * send_size, send_size)
        return pltpu.make_async_copy(outgoing.at[span], send_out.at[span], send_sem.at[part])

    tables = [
        pltpu.make_async_copy(far, near, table_sem.at[which])
        for which, (far, near) in enumerate(
            ((holder_far, holder_ref), (fresh_far, fresh_ref), (next_far, next_ref))
        )
    ]
    for copy in tables:
        copy.start()
    for tile in range(tiles):
        for copy in loads(tile):
            copy.start()
    for copy in tables:
        copy.wait()

    def add_slot(slot, total):
        total = jnp.where(fresh_ref[slot] > 0, 0.0, total) + pieces[slot].astype(jnp.float32)
        sums[pl.ds(holder_ref[slot] * pitch, height), :] = total
        return total

    lax.fori_loop(0, slots, add_slot, jnp.zeros((height, LANES), jnp.float32), unroll=4)

    @pl.loop(0, tiles)
    def _(tile):
        for copy in loads(tile):
            copy.wait()
        rows = pl.ds(pl.multiple_of(tile * deep, deep), deep)

        @pl.loop(0, blocks // GROUP)
        def _(four):
            for k in range(quad):
                block, row = divmod(k, share)
                place = pl.ds(tile * (deep * pitch) + four * quad + k, deep, stride=pitch)
                lanes = pl.ds(pl.multiple_of((four * GROUP + block) * LANES, LANES), LANES)
                grad = sums[place, :]
                first = (
                    BETA_ONE * one[row, rows, lanes].astype(jnp.float32)
                    + (1.0 - BETA_ONE) * grad
                )
                second = (
                    BETA_TWO * two[row, rows, lanes].astype(jnp.float32)
                    + (1.0 - BETA_TWO) * (grad * grad)
                )
                root = second * lax.rsqrt(second) + EPSILON * BIAS_TWO**0.5
                new = (1.0 - LEARN_RATE * DECAY_RATE) * master[row, rows, lanes] - (
                    (LEARN_RATE / BIAS_ONE * BIAS_TWO**0.5) * first
                ) / root
                master[row, rows, lanes] = new
                one[row, rows, lanes] = first.astype(jnp.bfloat16)
                two[row, rows, lanes] = second.astype(jnp.bfloat16)
                sums[place, :] = new

        for copy in stores(tile):
            copy.start()

    for part in range(sends):

        def fill(slot, carry):
            outgoing[slot] = sums[pl.ds(next_ref[slot] * pitch, height), :].astype(jnp.bfloat16)
            return carry

        lax.fori_loop(part * send_size, (part + 1) * send_size, fill, 0, unroll=4)
        send(part).start()

    for tile in range(tiles):
        for copy in stores(tile):
            copy.wait()
    for part in range(sends):
        send(part).wait()


def adam_step(holder, fresh, next_map, pieces, master, one, two, sends=4):
    slots, height, _ = pieces.shape
    share, experts, width = master.shape
    tiles = experts // 16
    return pl.pallas_call(
        adam_kernel,
        out_shape=(
            pltpu.HBM(master.shape, jnp.float32),
            pltpu.HBM(one.shape, jnp.bfloat16),
            pltpu.HBM(two.shape, jnp.bfloat16),
            pltpu.HBM((slots, height, LANES), jnp.bfloat16),
        ),
        in_specs=[FAR] * 3 + [NEAR] + [FAR] * 3,
        out_specs=(FAR,) * 4,
        scratch_shapes=[
            pltpu.SMEM((slots,), jnp.int32),
            pltpu.SMEM((slots,), jnp.int32),
            pltpu.SMEM((slots,), jnp.int32),
            pltpu.VMEM((experts * (height + 1), LANES), jnp.float32),
            pltpu.VMEM(master.shape, jnp.float32),
            pltpu.VMEM(one.shape, jnp.bfloat16),
            pltpu.VMEM(two.shape, jnp.bfloat16),
            pltpu.VMEM(pieces.shape, jnp.bfloat16),
            pltpu.SemaphoreType.DMA((3,)),
            pltpu.SemaphoreType.DMA((3, tiles)),
            pltpu.SemaphoreType.DMA((3, tiles)),
            pltpu.SemaphoreType.DMA((sends,)),
        ],
        compiler_params=pltpu.CompilerParams(vmem_limit_bytes=60 << 20),
        name="adam_step",
    )(
        holder, fresh, next_map, pltpu.with_memory_space_constraint(pieces, pltpu.VMEM),
        master, one, two,
    )


def rows_kernel(arrived, out_ref, wholes, tall, out_sem):
    slots, depth, _ = arrived.shape
    width = out_ref.shape[1]
    blocks = width // LANES
    share = depth // blocks
    height = tall.shape[1]
    members = height // share
    parts = out_sem.shape[0]
    part_size = slots // parts

    def store(part):
        span = pl.ds(part * part_size * share, part_size * share)
        return pltpu.make_async_copy(wholes.at[span], out_ref.at[span], out_sem.at[part])

    for part in range(parts):

        @pl.loop(part * part_size // members, (part + 1) * part_size // members)
        def _(group):
            base = pl.multiple_of(group * height, 16)
            for member in range(members):
                chunk = arrived[group * members + member].astype(jnp.float32)
                for block in range(blocks):
                    tall[block, member * share : (member + 1) * share, :] = chunk[
                        block * share : (block + 1) * share, :
                    ]
            for block in range(blocks):
                wholes[pl.ds(base, height), block * LANES : (block + 1) * LANES] = tall[
                    block
                ].astype(jnp.bfloat16)

        store(part).start()
    for part in range(parts):
        store(part).wait()


def chunk_rows(arrived, hidden, width, parts=8, members=8):
    slots, height, _ = arrived.shape
    blocks = width // LANES
    share = height // blocks
    return pl.pallas_call(
        rows_kernel,
        out_shape=jax.ShapeDtypeStruct((hidden, width), jnp.bfloat16),
        in_specs=[NEAR],
        out_specs=FAR,
        scratch_shapes=[
            pltpu.VMEM((hidden, width), jnp.bfloat16),
            pltpu.VMEM((blocks, members * share, LANES), jnp.float32),
            pltpu.SemaphoreType.DMA((parts,)),
        ],
        compiler_params=pltpu.CompilerParams(vmem_limit_bytes=32 << 20),
        name="chunk_rows",
    )(pltpu.with_memory_space_constraint(arrived, pltpu.VMEM))


def exchange(chunks):
    return lax.all_to_all(chunks, "dev", split_axis=0, concat_axis=0, tiled=True)


def per_device(saved, cotangent, weights, counts, live_rows, next_map, master, moment1, moment2):
    cot_rows = cotangent[0]
    devices = lax.axis_size("dev")
    experts, share, width = master.shape
    hidden = saved.shape[2]
    chunks = slot_chunks(saved[0], cot_rows, live_rows, devices)
    received = exchange(chunks)
    input_grads = input_rows(cot_rows, weights[0], live_rows)
    slot_index = jnp.arange(devices, dtype=jnp.int32)
    bounds = jnp.cumsum(counts)
    holders = jnp.sum((bounds[None, :] <= slot_index[:, None]).astype(jnp.int32), axis=1)
    fresh = jnp.any(bounds[None, :] == slot_index[:, None], axis=1) | (slot_index == 0)
    new_master, new_one, new_two, outgoing = adam_step(
        holders, fresh.astype(jnp.int32), next_map, received,
        master.transpose(1, 0, 2), moment1.transpose(1, 0, 2), moment2.transpose(1, 0, 2),
    )
    arriving = exchange(outgoing)
    next_weights = chunk_rows(arriving, hidden, width)
    return (
        input_grads[None],
        new_master.transpose(1, 0, 2),
        new_one.transpose(1, 0, 2),
        new_two.transpose(1, 0, 2),
        next_weights[None],
    )


def solution(mesh):
    placed = (
        P("dev", None, None),
        P("dev", None, None),
        P("dev", None, None),
        P(),
        P("dev"),
        P(),
        P(None, "dev", None),
        P(None, "dev", None),
        P(None, "dev", None),
    )
    return jax.shard_map(
        per_device,
        mesh=mesh,
        in_specs=placed,
        out_specs=(
            P("dev", None, None),
            P(None, "dev", None),
            P(None, "dev", None),
            P(None, "dev", None),
            P("dev", None, None),
        ),
        check_vma=False,
    )
```

```python
import functools
import jax
import jax.numpy as jnp
from jax import lax
from jax.experimental import pallas as pl
from jax.experimental.pallas import tpu as pltpu
from jax.sharding import PartitionSpec as P

LEARN_RATE = 0.001
DECAY_RATE = 0.1
BETA_ONE = 0.9
BETA_TWO = 0.95
BIAS_ONE = 1.0 - 0.9**20
BIAS_TWO = 1.0 - 0.95**20
EPSILON = 1e-08

LANES = 128
GROUP = 4


def contract_cols(left, right):
    return lax.dot_general(
        left, right, (((1,), (1,)), ((), ())), preferred_element_type=jnp.float32
    )


FAR = pl.BlockSpec(memory_space=pltpu.HBM)
NEAR = pl.BlockSpec(memory_space=pltpu.VMEM)
SCALARS = pl.BlockSpec(memory_space=pltpu.SMEM)


def grads_kernel(
    live_ref, saved_ref, cot_ref, out_ref,
    saved_in, cot_in, turned, ordered, packed, saved_sem, cot_sem, out_sem,
):
    rows, hidden = saved_ref.shape
    strips, _, thin = cot_in.shape
    steps = packed.shape[0]
    per_step = strips // steps
    devices = out_ref.shape[0]
    share = hidden // devices
    tall = ordered.shape[1]
    bands = saved_sem.shape[0]
    band_rows = rows // bands

    def load_saved(band):
        span = pl.ds(band * band_rows, band_rows)
        return pltpu.make_async_copy(saved_ref.at[span], saved_in.at[span], saved_sem.at[band])

    def load_cot(strip):
        span = pl.ds(strip * thin, thin)
        return pltpu.make_async_copy(cot_ref.at[:, span], cot_in.at[strip], cot_sem.at[strip])

    def send(step):
        span = pl.ds(pl.multiple_of(step * tall, tall), tall)
        return pltpu.make_async_copy(packed.at[step], out_ref.at[:, span], out_sem.at[step])

    def multiply(step, target):
        for which in range(per_step):
            strip = step * per_step + which
            pltpu.make_async_copy(
                cot_ref.at[:, :thin], cot_in.at[strip], cot_sem.at[strip]
            ).wait()
        for which in range(per_step):
            product = jnp.dot(
                turned[...], cot_in[step * per_step + which], preferred_element_type=jnp.float32
            )
            for part in range(thin // LANES):
                block = which * (thin // LANES) + part
                for device in range(devices):
                    target[device, block * share : (block + 1) * share, :] = product[
                        device * share : (device + 1) * share, part * LANES : (part + 1) * LANES
                    ]

    for band in range(bands):
        load_saved(band).start()

    @pl.loop(0, bands)
    def _(band):
        span = pl.ds(pl.multiple_of(band * band_rows, band_rows), band_rows)
        pltpu.make_async_copy(saved_ref.at[span], saved_in.at[span], saved_sem.at[band]).wait()

        @pl.when(band == 0)
        def _():
            for strip in range(per_step):
                load_cot(strip).start()

        index = lax.broadcasted_iota(jnp.int32, (band_rows, hidden), 0)
        part = saved_in[span, :]
        turned[:, span] = jnp.where(
            index < live_ref[0] - band * band_rows, part, jnp.zeros_like(part)
        ).T

    for strip in range(per_step, strips):
        load_cot(strip).start()

    @pl.loop(0, steps)
    def _(step):
        before = lax.rem(step + steps - 1, steps)
        for device in range(devices):
            packed[before, device] = ordered[device].astype(jnp.bfloat16)
        multiply(step, ordered)

        @pl.when(step > 0)
        def _():
            send(before).start()

    @pl.loop(0, devices // 8)
    def _(eight):
        for member in range(8):
            packed[steps - 1, eight * 8 + member] = ordered[eight * 8 + member].astype(
                jnp.bfloat16
            )

    send(steps - 1).start()
    for step in range(steps):
        send(step).wait()


def slot_chunks(saved, cot, live, devices, steps=4, bands=2):
    rows, hidden = saved.shape
    width = cot.shape[1]
    thin = 2 * LANES
    strips = width // thin
    share = hidden // devices
    blocks = width // LANES
    tall = blocks // steps * share
    return pl.pallas_call(
        grads_kernel,
        out_shape=jax.ShapeDtypeStruct((devices, blocks * share, LANES), jnp.bfloat16),
        in_specs=[SCALARS, FAR, FAR],
        out_specs=FAR,
        scratch_shapes=[
            pltpu.VMEM((rows, hidden), jnp.bfloat16),
            pltpu.VMEM((strips, rows, thin), jnp.bfloat16),
            pltpu.VMEM((hidden, rows), jnp.bfloat16),
            pltpu.VMEM((devices, tall, LANES), jnp.float32),
            pltpu.VMEM((steps, devices, tall, LANES), jnp.bfloat16),
            pltpu.SemaphoreType.DMA((bands,)),
            pltpu.SemaphoreType.DMA((strips,)),
            pltpu.SemaphoreType.DMA((steps,)),
        ],
        compiler_params=pltpu.CompilerParams(vmem_limit_bytes=63 << 20),
        cost_estimate=pl.CostEstimate(
            flops=2 * rows * hidden * width,
            bytes_accessed=2 * (rows * hidden + rows * width + hidden * width),
            transcendentals=0,
        ),
        name="slot_chunks",
    )(live, saved, cot)


def inputs_kernel(live_ref, cot_ref, weights_ref, out_ref):
    tall = cot_ref.shape[0]
    index = lax.broadcasted_iota(jnp.int32, out_ref.shape, 0) + pl.program_id(0) * tall
    product = contract_cols(cot_ref[...], weights_ref[...])
    out_ref[...] = jnp.where(index < live_ref[0], product, 0.0).astype(jnp.bfloat16)


def input_rows(cot, weights, live, steps=4):
    rows, width = cot.shape
    hidden = weights.shape[0]
    return pl.pallas_call(
        inputs_kernel,
        out_shape=jax.ShapeDtypeStruct((rows, hidden), jnp.bfloat16),
        grid=(steps,),
        in_specs=[
            SCALARS,
            pl.BlockSpec((rows // steps, width), lambda i: (i, 0)),
            pl.BlockSpec((hidden, width), lambda i: (0, 0)),
        ],
        out_specs=pl.BlockSpec((rows // steps, hidden), lambda i: (i, 0)),
        compiler_params=pltpu.CompilerParams(
            dimension_semantics=("arbitrary",), vmem_limit_bytes=40 << 20
        ),
        cost_estimate=pl.CostEstimate(
            flops=2 * rows * hidden * width,
            bytes_accessed=2 * (rows * hidden + rows * width + hidden * width),
            transcendentals=0,
        ),
        name="input_rows",
    )(live, cot, weights)


def adam_kernel(
    holder_far, fresh_far, next_far, pieces, master_ref, one_ref, two_ref,
    master_out, one_out, two_out, send_out,
    holder_ref, fresh_ref, next_ref, sums, master, one, two, outgoing,
    table_sem, load_sem, store_sem, send_sem,
):
    slots, height, _ = pieces.shape
    share, experts, width = master_ref.shape
    blocks = width // LANES
    deep = 16
    tiles = experts // deep
    quad = GROUP * share
    pitch = sums.shape[0] // experts
    arrays = ((master_ref, master, master_out), (one_ref, one, one_out), (two_ref, two, two_out))
    sends = send_sem.shape[0]
    send_size = slots // sends

    def loads(tile):
        span = pl.ds(pl.multiple_of(tile * deep, deep), deep)
        return [
            pltpu.make_async_copy(far.at[:, span, :], near.at[:, span, :], load_sem.at[which, tile])
            for which, (far, near, _) in enumerate(arrays)
        ]

    def stores(tile):
        span = pl.ds(pl.multiple_of(tile * deep, deep), deep)
        return [
            pltpu.make_async_copy(near.at[:, span, :], far.at[:, span, :], store_sem.at[which, tile])
            for which, (_, near, far) in enumerate(arrays)
        ]

    def send(part):
        span = pl.ds(part * send_size, send_size)
        return pltpu.make_async_copy(outgoing.at[span], send_out.at[span], send_sem.at[part])

    tables = [
        pltpu.make_async_copy(far, near, table_sem.at[which])
        for which, (far, near) in enumerate(
            ((holder_far, holder_ref), (fresh_far, fresh_ref), (next_far, next_ref))
        )
    ]
    for copy in tables:
        copy.start()
    for tile in range(tiles):
        for copy in loads(tile):
            copy.start()
    for copy in tables:
        copy.wait()

    def add_slot(slot, total):
        total = jnp.where(fresh_ref[slot] > 0, 0.0, total) + pieces[slot].astype(jnp.float32)
        sums[pl.ds(holder_ref[slot] * pitch, height), :] = total
        return total

    lax.fori_loop(0, slots, add_slot, jnp.zeros((height, LANES), jnp.float32), unroll=4)

    @pl.loop(0, tiles)
    def _(tile):
        for copy in loads(tile):
            copy.wait()
        rows = pl.ds(pl.multiple_of(tile * deep, deep), deep)

        @pl.loop(0, blocks // GROUP)
        def _(four):
            for k in range(quad):
                block, row = divmod(k, share)
                place = pl.ds(tile * (deep * pitch) + four * quad + k, deep, stride=pitch)
                lanes = pl.ds(pl.multiple_of((four * GROUP + block) * LANES, LANES), LANES)
                grad = sums[place, :]
                first = (
                    BETA_ONE * one[row, rows, lanes].astype(jnp.float32)
                    + (1.0 - BETA_ONE) * grad
                )
                second = (
                    BETA_TWO * two[row, rows, lanes].astype(jnp.float32)
                    + (1.0 - BETA_TWO) * (grad * grad)
                )
                root = second * lax.rsqrt(second) + EPSILON * BIAS_TWO**0.5
                new = (1.0 - LEARN_RATE * DECAY_RATE) * master[row, rows, lanes] - (
                    (LEARN_RATE / BIAS_ONE * BIAS_TWO**0.5) * first
                ) / root
                master[row, rows, lanes] = new
                one[row, rows, lanes] = first.astype(jnp.bfloat16)
                two[row, rows, lanes] = second.astype(jnp.bfloat16)
                sums[place, :] = new

        for copy in stores(tile):
            copy.start()

    for part in range(sends):

        def fill(slot, carry):
            outgoing[slot] = sums[pl.ds(next_ref[slot] * pitch, height), :].astype(jnp.bfloat16)
            return carry

        lax.fori_loop(part * send_size, (part + 1) * send_size, fill, 0, unroll=4)
        send(part).start()

    for tile in range(tiles):
        for copy in stores(tile):
            copy.wait()
    for part in range(sends):
        send(part).wait()


def adam_step(holder, fresh, next_map, pieces, master, one, two, sends=4):
    slots, height, _ = pieces.shape
    share, experts, width = master.shape
    tiles = experts // 16
    return pl.pallas_call(
        adam_kernel,
        out_shape=(
            pltpu.HBM(master.shape, jnp.float32),
            pltpu.HBM(one.shape, jnp.bfloat16),
            pltpu.HBM(two.shape, jnp.bfloat16),
            pltpu.HBM((slots, height, LANES), jnp.bfloat16),
        ),
        in_specs=[FAR] * 3 + [NEAR] + [FAR] * 3,
        out_specs=(FAR,) * 4,
        scratch_shapes=[
            pltpu.SMEM((slots,), jnp.int32),
            pltpu.SMEM((slots,), jnp.int32),
            pltpu.SMEM((slots,), jnp.int32),
            pltpu.VMEM((experts * (height + 1), LANES), jnp.float32),
            pltpu.VMEM(master.shape, jnp.float32),
            pltpu.VMEM(one.shape, jnp.bfloat16),
            pltpu.VMEM(two.shape, jnp.bfloat16),
            pltpu.VMEM(pieces.shape, jnp.bfloat16),
            pltpu.SemaphoreType.DMA((3,)),
            pltpu.SemaphoreType.DMA((3, tiles)),
            pltpu.SemaphoreType.DMA((3, tiles)),
            pltpu.SemaphoreType.DMA((sends,)),
        ],
        compiler_params=pltpu.CompilerParams(vmem_limit_bytes=60 << 20),
        name="adam_step",
    )(
        holder, fresh, next_map, pltpu.with_memory_space_constraint(pieces, pltpu.VMEM),
        master, one, two,
    )


def rows_kernel(arrived, out_ref, wholes, tall, out_sem):
    slots, depth, _ = arrived.shape
    width = out_ref.shape[1]
    blocks = width // LANES
    share = depth // blocks
    height = tall.shape[1]
    members = height // share
    parts = out_sem.shape[0]
    part_size = slots // parts

    def store(part):
        span = pl.ds(part * part_size * share, part_size * share)
        return pltpu.make_async_copy(wholes.at[span], out_ref.at[span], out_sem.at[part])

    for part in range(parts):

        @pl.loop(part * part_size // members, (part + 1) * part_size // members)
        def _(group):
            base = pl.multiple_of(group * height, 16)
            for member in range(members):
                chunk = arrived[group * members + member].astype(jnp.float32)
                for block in range(blocks):
                    tall[block, member * share : (member + 1) * share, :] = chunk[
                        block * share : (block + 1) * share, :
                    ]
            for block in range(blocks):
                wholes[pl.ds(base, height), block * LANES : (block + 1) * LANES] = tall[
                    block
                ].astype(jnp.bfloat16)

        store(part).start()
    for part in range(parts):
        store(part).wait()


def chunk_rows(arrived, hidden, width, parts=8, members=8):
    slots, height, _ = arrived.shape
    blocks = width // LANES
    share = height // blocks
    return pl.pallas_call(
        rows_kernel,
        out_shape=jax.ShapeDtypeStruct((hidden, width), jnp.bfloat16),
        in_specs=[NEAR],
        out_specs=FAR,
        scratch_shapes=[
            pltpu.VMEM((hidden, width), jnp.bfloat16),
            pltpu.VMEM((blocks, members * share, LANES), jnp.float32),
            pltpu.SemaphoreType.DMA((parts,)),
        ],
        compiler_params=pltpu.CompilerParams(vmem_limit_bytes=32 << 20),
        name="chunk_rows",
    )(pltpu.with_memory_space_constraint(arrived, pltpu.VMEM))


def exchange(chunks):
    return lax.all_to_all(chunks, "dev", split_axis=0, concat_axis=0, tiled=True)


def per_device(saved, cotangent, weights, counts, live_rows, next_map, master, moment1, moment2):
    cot_rows = cotangent[0]
    devices = lax.axis_size("dev")
    experts, share, width = master.shape
    hidden = saved.shape[2]
    chunks = slot_chunks(saved[0], cot_rows, live_rows, devices)
    received = exchange(chunks)
    input_grads = input_rows(cot_rows, weights[0], live_rows)
    slot_index = jnp.arange(devices, dtype=jnp.int32)
    bounds = jnp.cumsum(counts)
    holders = jnp.sum((bounds[None, :] <= slot_index[:, None]).astype(jnp.int32), axis=1)
    fresh = jnp.any(bounds[None, :] == slot_index[:, None], axis=1) | (slot_index == 0)
    new_master, new_one, new_two, outgoing = adam_step(
        holders, fresh.astype(jnp.int32), next_map, received,
        master.transpose(1, 0, 2), moment1.transpose(1, 0, 2), moment2.transpose(1, 0, 2),
    )
    arriving = exchange(outgoing)
    next_weights = chunk_rows(arriving, hidden, width)
    return (
        input_grads[None],
        new_master.transpose(1, 0, 2),
        new_one.transpose(1, 0, 2),
        new_two.transpose(1, 0, 2),
        next_weights[None],
    )


def solution(mesh):
    placed = (
        P("dev", None, None),
        P("dev", None, None),
        P("dev", None, None),
        P(),
        P("dev"),
        P(),
        P(None, "dev", None),
        P(None, "dev", None),
        P(None, "dev", None),
    )
    return jax.shard_map(
        per_device,
        mesh=mesh,
        in_specs=placed,
        out_specs=(
            P("dev", None, None),
            P(None, "dev", None),
            P(None, "dev", None),
            P(None, "dev", None),
            P("dev", None, None),
        ),
        check_vma=False,
    )
```

```python
import functools
import jax
import jax.numpy as jnp
from jax import lax
from jax.experimental import pallas as pl
from jax.experimental.pallas import tpu as pltpu
from jax.sharding import PartitionSpec as P

LEARN_RATE = 0.001
DECAY_RATE = 0.1
BETA_ONE = 0.9
BETA_TWO = 0.95
BIAS_ONE = 1.0 - 0.9**20
BIAS_TWO = 1.0 - 0.95**20
EPSILON = 1e-08

LANES = 128
GROUP = 4


def contract_cols(left, right):
    return lax.dot_general(
        left, right, (((1,), (1,)), ((), ())), preferred_element_type=jnp.float32
    )


FAR = pl.BlockSpec(memory_space=pltpu.HBM)
NEAR = pl.BlockSpec(memory_space=pltpu.VMEM)
SCALARS = pl.BlockSpec(memory_space=pltpu.SMEM)


def grads_kernel(
    live_ref, saved_ref, cot_ref, out_ref,
    saved_in, cot_in, turned, ordered, packed, saved_sem, cot_sem, out_sem,
):
    rows, hidden = saved_ref.shape
    strips, _, thin = cot_in.shape
    steps = packed.shape[0]
    per_step = strips // steps
    devices = out_ref.shape[0]
    share = hidden // devices
    tall = ordered.shape[1]
    bands = saved_sem.shape[0]
    band_rows = rows // bands

    def load_saved(band):
        span = pl.ds(band * band_rows, band_rows)
        return pltpu.make_async_copy(saved_ref.at[span], saved_in.at[span], saved_sem.at[band])

    def load_cot(strip):
        span = pl.ds(strip * thin, thin)
        return pltpu.make_async_copy(cot_ref.at[:, span], cot_in.at[strip], cot_sem.at[strip])

    def send(step):
        span = pl.ds(pl.multiple_of(step * tall, tall), tall)
        return pltpu.make_async_copy(packed.at[step], out_ref.at[:, span], out_sem.at[step])

    def multiply(step, target):
        for which in range(per_step):
            strip = step * per_step + which
            pltpu.make_async_copy(
                cot_ref.at[:, :thin], cot_in.at[strip], cot_sem.at[strip]
            ).wait()
        for which in range(per_step):
            product = jnp.dot(
                turned[...], cot_in[step * per_step + which], preferred_element_type=jnp.float32
            )
            for part in range(thin // LANES):
                block = which * (thin // LANES) + part
                for device in range(devices):
                    target[device, block * share : (block + 1) * share, :] = product[
                        device * share : (device + 1) * share, part * LANES : (part + 1) * LANES
                    ]

    for band in range(bands):
        load_saved(band).start()
    for strip in range(per_step):
        load_cot(strip).start()

    @pl.loop(0, bands)
    def _(band):
        span = pl.ds(pl.multiple_of(band * band_rows, band_rows), band_rows)
        pltpu.make_async_copy(saved_ref.at[span], saved_in.at[span], saved_sem.at[band]).wait()

        index = lax.broadcasted_iota(jnp.int32, (band_rows, hidden), 0)
        part = saved_in[span, :]
        turned[:, span] = jnp.where(
            index < live_ref[0] - band * band_rows, part, jnp.zeros_like(part)
        ).T

    for strip in range(per_step, strips):
        load_cot(strip).start()

    @pl.loop(0, steps)
    def _(step):
        before = lax.rem(step + steps - 1, steps)
        for device in range(devices):
            packed[before, device] = ordered[device].astype(jnp.bfloat16)
        multiply(step, ordered)

        @pl.when(step > 0)
        def _():
            send(before).start()

    @pl.loop(0, devices // 8)
    def _(eight):
        for member in range(8):
            packed[steps - 1, eight * 8 + member] = ordered[eight * 8 + member].astype(
                jnp.bfloat16
            )

    send(steps - 1).start()
    for step in range(steps):
        send(step).wait()


def slot_chunks(saved, cot, live, devices, steps=4, bands=2):
    rows, hidden = saved.shape
    width = cot.shape[1]
    thin = 2 * LANES
    strips = width // thin
    share = hidden // devices
    blocks = width // LANES
    tall = blocks // steps * share
    return pl.pallas_call(
        grads_kernel,
        out_shape=jax.ShapeDtypeStruct((devices, blocks * share, LANES), jnp.bfloat16),
        in_specs=[SCALARS, FAR, FAR],
        out_specs=FAR,
        scratch_shapes=[
            pltpu.VMEM((rows, hidden), jnp.bfloat16),
            pltpu.VMEM((strips, rows, thin), jnp.bfloat16),
            pltpu.VMEM((hidden, rows), jnp.bfloat16),
            pltpu.VMEM((devices, tall, LANES), jnp.float32),
            pltpu.VMEM((steps, devices, tall, LANES), jnp.bfloat16),
            pltpu.SemaphoreType.DMA((bands,)),
            pltpu.SemaphoreType.DMA((strips,)),
            pltpu.SemaphoreType.DMA((steps,)),
        ],
        compiler_params=pltpu.CompilerParams(vmem_limit_bytes=63 << 20),
        cost_estimate=pl.CostEstimate(
            flops=2 * rows * hidden * width,
            bytes_accessed=2 * (rows * hidden + rows * width + hidden * width),
            transcendentals=0,
        ),
        name="slot_chunks",
    )(live, saved, cot)


def inputs_kernel(live_ref, cot_ref, weights_ref, out_ref):
    tall = cot_ref.shape[0]
    index = lax.broadcasted_iota(jnp.int32, out_ref.shape, 0) + pl.program_id(0) * tall
    product = contract_cols(cot_ref[...], weights_ref[...])
    out_ref[...] = jnp.where(index < live_ref[0], product, 0.0).astype(jnp.bfloat16)


def input_rows(cot, weights, live, steps=4):
    rows, width = cot.shape
    hidden = weights.shape[0]
    return pl.pallas_call(
        inputs_kernel,
        out_shape=jax.ShapeDtypeStruct((rows, hidden), jnp.bfloat16),
        grid=(steps,),
        in_specs=[
            SCALARS,
            pl.BlockSpec((rows // steps, width), lambda i: (i, 0)),
            pl.BlockSpec((hidden, width), lambda i: (0, 0)),
        ],
        out_specs=pl.BlockSpec((rows // steps, hidden), lambda i: (i, 0)),
        compiler_params=pltpu.CompilerParams(
            dimension_semantics=("arbitrary",), vmem_limit_bytes=40 << 20
        ),
        cost_estimate=pl.CostEstimate(
            flops=2 * rows * hidden * width,
            bytes_accessed=2 * (rows * hidden + rows * width + hidden * width),
            transcendentals=0,
        ),
        name="input_rows",
    )(live, cot, weights)


def adam_kernel(
    holder_far, fresh_far, next_far, pieces, master_ref, one_ref, two_ref,
    master_out, one_out, two_out, send_out,
    holder_ref, fresh_ref, next_ref, sums, master, one, two, outgoing,
    table_sem, load_sem, store_sem, send_sem,
):
    slots, height, _ = pieces.shape
    share, experts, width = master_ref.shape
    blocks = width // LANES
    deep = 16
    tiles = experts // deep
    quad = GROUP * share
    pitch = sums.shape[0] // experts
    arrays = ((master_ref, master, master_out), (one_ref, one, one_out), (two_ref, two, two_out))
    sends = send_sem.shape[0]
    send_size = slots // sends

    def loads(tile):
        span = pl.ds(pl.multiple_of(tile * deep, deep), deep)
        return [
            pltpu.make_async_copy(far.at[:, span, :], near.at[:, span, :], load_sem.at[which, tile])
            for which, (far, near, _) in enumerate(arrays)
        ]

    def stores(tile):
        span = pl.ds(pl.multiple_of(tile * deep, deep), deep)
        return [
            pltpu.make_async_copy(near.at[:, span, :], far.at[:, span, :], store_sem.at[which, tile])
            for which, (_, near, far) in enumerate(arrays)
        ]

    def send(part):
        span = pl.ds(part * send_size, send_size)
        return pltpu.make_async_copy(outgoing.at[span], send_out.at[span], send_sem.at[part])

    tables = [
        pltpu.make_async_copy(far, near, table_sem.at[which])
        for which, (far, near) in enumerate(
            ((holder_far, holder_ref), (fresh_far, fresh_ref), (next_far, next_ref))
        )
    ]
    for copy in tables:
        copy.start()
    for tile in range(tiles):
        for copy in loads(tile):
            copy.start()
    for copy in tables:
        copy.wait()

    def add_slot(slot, total):
        total = jnp.where(fresh_ref[slot] > 0, 0.0, total) + pieces[slot].astype(jnp.float32)
        sums[pl.ds(holder_ref[slot] * pitch, height), :] = total
        return total

    lax.fori_loop(0, slots, add_slot, jnp.zeros((height, LANES), jnp.float32), unroll=4)

    @pl.loop(0, tiles)
    def _(tile):
        for copy in loads(tile):
            copy.wait()
        rows = pl.ds(pl.multiple_of(tile * deep, deep), deep)

        @pl.loop(0, blocks // GROUP)
        def _(four):
            for k in range(quad):
                block, row = divmod(k, share)
                place = pl.ds(tile * (deep * pitch) + four * quad + k, deep, stride=pitch)
                lanes = pl.ds(pl.multiple_of((four * GROUP + block) * LANES, LANES), LANES)
                grad = sums[place, :]
                first = (
                    BETA_ONE * one[row, rows, lanes].astype(jnp.float32)
                    + (1.0 - BETA_ONE) * grad
                )
                second = (
                    BETA_TWO * two[row, rows, lanes].astype(jnp.float32)
                    + (1.0 - BETA_TWO) * (grad * grad)
                )
                root = second * lax.rsqrt(second) + EPSILON * BIAS_TWO**0.5
                new = (1.0 - LEARN_RATE * DECAY_RATE) * master[row, rows, lanes] - (
                    (LEARN_RATE / BIAS_ONE * BIAS_TWO**0.5) * first
                ) / root
                master[row, rows, lanes] = new
                one[row, rows, lanes] = first.astype(jnp.bfloat16)
                two[row, rows, lanes] = second.astype(jnp.bfloat16)
                sums[place, :] = new

        for copy in stores(tile):
            copy.start()

    for part in range(sends):

        def fill(slot, carry):
            outgoing[slot] = sums[pl.ds(next_ref[slot] * pitch, height), :].astype(jnp.bfloat16)
            return carry

        lax.fori_loop(part * send_size, (part + 1) * send_size, fill, 0, unroll=4)
        send(part).start()

    for tile in range(tiles):
        for copy in stores(tile):
            copy.wait()
    for part in range(sends):
        send(part).wait()


def adam_step(holder, fresh, next_map, pieces, master, one, two, sends=4):
    slots, height, _ = pieces.shape
    share, experts, width = master.shape
    tiles = experts // 16
    return pl.pallas_call(
        adam_kernel,
        out_shape=(
            pltpu.HBM(master.shape, jnp.float32),
            pltpu.HBM(one.shape, jnp.bfloat16),
            pltpu.HBM(two.shape, jnp.bfloat16),
            pltpu.HBM((slots, height, LANES), jnp.bfloat16),
        ),
        in_specs=[FAR] * 3 + [NEAR] + [FAR] * 3,
        out_specs=(FAR,) * 4,
        scratch_shapes=[
            pltpu.SMEM((slots,), jnp.int32),
            pltpu.SMEM((slots,), jnp.int32),
            pltpu.SMEM((slots,), jnp.int32),
            pltpu.VMEM((experts * (height + 1), LANES), jnp.float32),
            pltpu.VMEM(master.shape, jnp.float32),
            pltpu.VMEM(one.shape, jnp.bfloat16),
            pltpu.VMEM(two.shape, jnp.bfloat16),
            pltpu.VMEM(pieces.shape, jnp.bfloat16),
            pltpu.SemaphoreType.DMA((3,)),
            pltpu.SemaphoreType.DMA((3, tiles)),
            pltpu.SemaphoreType.DMA((3, tiles)),
            pltpu.SemaphoreType.DMA((sends,)),
        ],
        compiler_params=pltpu.CompilerParams(vmem_limit_bytes=60 << 20),
        name="adam_step",
    )(
        holder, fresh, next_map, pltpu.with_memory_space_constraint(pieces, pltpu.VMEM),
        master, one, two,
    )


def rows_kernel(arrived, out_ref, wholes, tall, out_sem):
    slots, depth, _ = arrived.shape
    width = out_ref.shape[1]
    blocks = width // LANES
    share = depth // blocks
    height = tall.shape[1]
    members = height // share
    parts = out_sem.shape[0]
    part_size = slots // parts

    def store(part):
        span = pl.ds(part * part_size * share, part_size * share)
        return pltpu.make_async_copy(wholes.at[span], out_ref.at[span], out_sem.at[part])

    for part in range(parts):

        @pl.loop(part * part_size // members, (part + 1) * part_size // members)
        def _(group):
            base = pl.multiple_of(group * height, 16)
            for member in range(members):
                chunk = arrived[group * members + member].astype(jnp.float32)
                for block in range(blocks):
                    tall[block, member * share : (member + 1) * share, :] = chunk[
                        block * share : (block + 1) * share, :
                    ]
            for block in range(blocks):
                wholes[pl.ds(base, height), block * LANES : (block + 1) * LANES] = tall[
                    block
                ].astype(jnp.bfloat16)

        store(part).start()
    for part in range(parts):
        store(part).wait()


def chunk_rows(arrived, hidden, width, parts=8, members=8):
    slots, height, _ = arrived.shape
    blocks = width // LANES
    share = height // blocks
    return pl.pallas_call(
        rows_kernel,
        out_shape=jax.ShapeDtypeStruct((hidden, width), jnp.bfloat16),
        in_specs=[NEAR],
        out_specs=FAR,
        scratch_shapes=[
            pltpu.VMEM((hidden, width), jnp.bfloat16),
            pltpu.VMEM((blocks, members * share, LANES), jnp.float32),
            pltpu.SemaphoreType.DMA((parts,)),
        ],
        compiler_params=pltpu.CompilerParams(vmem_limit_bytes=32 << 20),
        name="chunk_rows",
    )(pltpu.with_memory_space_constraint(arrived, pltpu.VMEM))


def exchange(chunks):
    return lax.all_to_all(chunks, "dev", split_axis=0, concat_axis=0, tiled=True)


def per_device(saved, cotangent, weights, counts, live_rows, next_map, master, moment1, moment2):
    cot_rows = cotangent[0]
    devices = lax.axis_size("dev")
    experts, share, width = master.shape
    hidden = saved.shape[2]
    chunks = slot_chunks(saved[0], cot_rows, live_rows, devices)
    received = exchange(chunks)
    input_grads = input_rows(cot_rows, weights[0], live_rows)
    slot_index = jnp.arange(devices, dtype=jnp.int32)
    bounds = jnp.cumsum(counts)
    holders = jnp.sum((bounds[None, :] <= slot_index[:, None]).astype(jnp.int32), axis=1)
    fresh = jnp.any(bounds[None, :] == slot_index[:, None], axis=1) | (slot_index == 0)
    new_master, new_one, new_two, outgoing = adam_step(
        holders, fresh.astype(jnp.int32), next_map, received,
        master.transpose(1, 0, 2), moment1.transpose(1, 0, 2), moment2.transpose(1, 0, 2),
    )
    arriving = exchange(outgoing)
    next_weights = chunk_rows(arriving, hidden, width)
    return (
        input_grads[None],
        new_master.transpose(1, 0, 2),
        new_one.transpose(1, 0, 2),
        new_two.transpose(1, 0, 2),
        next_weights[None],
    )


def solution(mesh):
    placed = (
        P("dev", None, None),
        P("dev", None, None),
        P("dev", None, None),
        P(),
        P("dev"),
        P(),
        P(None, "dev", None),
        P(None, "dev", None),
        P(None, "dev", None),
    )
    return jax.shard_map(
        per_device,
        mesh=mesh,
        in_specs=placed,
        out_specs=(
            P("dev", None, None),
            P(None, "dev", None),
            P(None, "dev", None),
            P(None, "dev", None),
            P("dev", None, None),
        ),
        check_vma=False,
    )
```

```python
import functools
import jax
import jax.numpy as jnp
from jax import lax
from jax.experimental import pallas as pl
from jax.experimental.pallas import tpu as pltpu
from jax.sharding import PartitionSpec as P

LEARN_RATE = 0.001
DECAY_RATE = 0.1
BETA_ONE = 0.9
BETA_TWO = 0.95
BIAS_ONE = 1.0 - 0.9**20
BIAS_TWO = 1.0 - 0.95**20
EPSILON = 1e-08

LANES = 128
GROUP = 4


def contract_cols(left, right):
    return lax.dot_general(
        left, right, (((1,), (1,)), ((), ())), preferred_element_type=jnp.float32
    )


FAR = pl.BlockSpec(memory_space=pltpu.HBM)
NEAR = pl.BlockSpec(memory_space=pltpu.VMEM)
SCALARS = pl.BlockSpec(memory_space=pltpu.SMEM)


def grads_kernel(
    live_ref, saved_ref, cot_ref, out_ref,
    saved_in, cot_in, turned, ordered, packed, saved_sem, cot_sem, out_sem,
):
    rows, hidden = saved_ref.shape
    strips, _, thin = cot_in.shape
    steps = packed.shape[0]
    per_step = strips // steps
    devices = out_ref.shape[0]
    share = hidden // devices
    tall = ordered.shape[1]
    bands = saved_sem.shape[0]
    band_rows = rows // bands

    def load_saved(band):
        span = pl.ds(band * band_rows, band_rows)
        return pltpu.make_async_copy(saved_ref.at[span], saved_in.at[span], saved_sem.at[band])

    def load_cot(strip):
        span = pl.ds(strip * thin, thin)
        return pltpu.make_async_copy(cot_ref.at[:, span], cot_in.at[strip], cot_sem.at[strip])

    def send(step):
        span = pl.ds(pl.multiple_of(step * tall, tall), tall)
        return pltpu.make_async_copy(packed.at[step], out_ref.at[:, span], out_sem.at[step])

    def multiply(step, target):
        for which in range(per_step):
            strip = step * per_step + which
            pltpu.make_async_copy(
                cot_ref.at[:, :thin], cot_in.at[strip], cot_sem.at[strip]
            ).wait()
        for which in range(per_step):
            product = jnp.dot(
                turned[...], cot_in[step * per_step + which], preferred_element_type=jnp.float32
            )
            for part in range(thin // LANES):
                block = which * (thin // LANES) + part
                for device in range(devices):
                    target[device, block * share : (block + 1) * share, :] = product[
                        device * share : (device + 1) * share, part * LANES : (part + 1) * LANES
                    ]

    for band in range(bands):
        load_saved(band).start()
    for strip in range(per_step):
        load_cot(strip).start()

    @pl.loop(0, bands)
    def _(band):
        span = pl.ds(pl.multiple_of(band * band_rows, band_rows), band_rows)
        pltpu.make_async_copy(saved_ref.at[span], saved_in.at[span], saved_sem.at[band]).wait()

        index = lax.broadcasted_iota(jnp.int32, (band_rows, hidden), 0)
        part = saved_in[span, :]
        turned[:, span] = jnp.where(
            index < live_ref[0] - band * band_rows, part, jnp.zeros_like(part)
        ).T

    for strip in range(per_step, strips):
        load_cot(strip).start()

    @pl.loop(0, steps)
    def _(step):
        before = lax.rem(step + steps - 1, steps)
        for device in range(devices):
            packed[before, device] = ordered[device].astype(jnp.bfloat16)
        multiply(step, ordered)

        @pl.when(step > 0)
        def _():
            send(before).start()

    @pl.loop(0, devices // 8)
    def _(eight):
        for member in range(8):
            packed[steps - 1, eight * 8 + member] = ordered[eight * 8 + member].astype(
                jnp.bfloat16
            )

    send(steps - 1).start()
    for step in range(steps):
        send(step).wait()


def slot_chunks(saved, cot, live, devices, steps=4, bands=4):
    rows, hidden = saved.shape
    width = cot.shape[1]
    thin = 2 * LANES
    strips = width // thin
    share = hidden // devices
    blocks = width // LANES
    tall = blocks // steps * share
    return pl.pallas_call(
        grads_kernel,
        out_shape=jax.ShapeDtypeStruct((devices, blocks * share, LANES), jnp.bfloat16),
        in_specs=[SCALARS, FAR, FAR],
        out_specs=FAR,
        scratch_shapes=[
            pltpu.VMEM((rows, hidden), jnp.bfloat16),
            pltpu.VMEM((strips, rows, thin), jnp.bfloat16),
            pltpu.VMEM((hidden, rows), jnp.bfloat16),
            pltpu.VMEM((devices, tall, LANES), jnp.float32),
            pltpu.VMEM((steps, devices, tall, LANES), jnp.bfloat16),
            pltpu.SemaphoreType.DMA((bands,)),
            pltpu.SemaphoreType.DMA((strips,)),
            pltpu.SemaphoreType.DMA((steps,)),
        ],
        compiler_params=pltpu.CompilerParams(vmem_limit_bytes=63 << 20),
        cost_estimate=pl.CostEstimate(
            flops=2 * rows * hidden * width,
            bytes_accessed=2 * (rows * hidden + rows * width + hidden * width),
            transcendentals=0,
        ),
        name="slot_chunks",
    )(live, saved, cot)


def inputs_kernel(live_ref, cot_ref, weights_ref, out_ref):
    tall = cot_ref.shape[0]
    index = lax.broadcasted_iota(jnp.int32, out_ref.shape, 0) + pl.program_id(0) * tall
    product = contract_cols(cot_ref[...], weights_ref[...])
    out_ref[...] = jnp.where(index < live_ref[0], product, 0.0).astype(jnp.bfloat16)


def input_rows(cot, weights, live, steps=4):
    rows, width = cot.shape
    hidden = weights.shape[0]
    return pl.pallas_call(
        inputs_kernel,
        out_shape=jax.ShapeDtypeStruct((rows, hidden), jnp.bfloat16),
        grid=(steps,),
        in_specs=[
            SCALARS,
            pl.BlockSpec((rows // steps, width), lambda i: (i, 0)),
            pl.BlockSpec((hidden, width), lambda i: (0, 0)),
        ],
        out_specs=pl.BlockSpec((rows // steps, hidden), lambda i: (i, 0)),
        compiler_params=pltpu.CompilerParams(
            dimension_semantics=("arbitrary",), vmem_limit_bytes=40 << 20
        ),
        cost_estimate=pl.CostEstimate(
            flops=2 * rows * hidden * width,
            bytes_accessed=2 * (rows * hidden + rows * width + hidden * width),
            transcendentals=0,
        ),
        name="input_rows",
    )(live, cot, weights)


def adam_kernel(
    holder_far, fresh_far, next_far, pieces, master_ref, one_ref, two_ref,
    master_out, one_out, two_out, send_out,
    holder_ref, fresh_ref, next_ref, sums, master, one, two, outgoing,
    table_sem, load_sem, store_sem, send_sem,
):
    slots, height, _ = pieces.shape
    share, experts, width = master_ref.shape
    blocks = width // LANES
    deep = 16
    tiles = experts // deep
    quad = GROUP * share
    pitch = sums.shape[0] // experts
    arrays = ((master_ref, master, master_out), (one_ref, one, one_out), (two_ref, two, two_out))
    sends = send_sem.shape[0]
    send_size = slots // sends

    def loads(tile):
        span = pl.ds(pl.multiple_of(tile * deep, deep), deep)
        return [
            pltpu.make_async_copy(far.at[:, span, :], near.at[:, span, :], load_sem.at[which, tile])
            for which, (far, near, _) in enumerate(arrays)
        ]

    def stores(tile):
        span = pl.ds(pl.multiple_of(tile * deep, deep), deep)
        return [
            pltpu.make_async_copy(near.at[:, span, :], far.at[:, span, :], store_sem.at[which, tile])
            for which, (_, near, far) in enumerate(arrays)
        ]

    def send(part):
        span = pl.ds(part * send_size, send_size)
        return pltpu.make_async_copy(outgoing.at[span], send_out.at[span], send_sem.at[part])

    tables = [
        pltpu.make_async_copy(far, near, table_sem.at[which])
        for which, (far, near) in enumerate(
            ((holder_far, holder_ref), (fresh_far, fresh_ref), (next_far, next_ref))
        )
    ]
    for copy in tables:
        copy.start()
    for tile in range(tiles):
        for copy in loads(tile):
            copy.start()
    for copy in tables:
        copy.wait()

    def add_slot(slot, total):
        total = jnp.where(fresh_ref[slot] > 0, 0.0, total) + pieces[slot].astype(jnp.float32)
        sums[pl.ds(holder_ref[slot] * pitch, height), :] = total
        return total

    lax.fori_loop(0, slots, add_slot, jnp.zeros((height, LANES), jnp.float32), unroll=4)

    @pl.loop(0, tiles)
    def _(tile):
        for copy in loads(tile):
            copy.wait()
        rows = pl.ds(pl.multiple_of(tile * deep, deep), deep)

        @pl.loop(0, blocks // GROUP)
        def _(four):
            for k in range(quad):
                block, row = divmod(k, share)
                place = pl.ds(tile * (deep * pitch) + four * quad + k, deep, stride=pitch)
                lanes = pl.ds(pl.multiple_of((four * GROUP + block) * LANES, LANES), LANES)
                grad = sums[place, :]
                first = (
                    BETA_ONE * one[row, rows, lanes].astype(jnp.float32)
                    + (1.0 - BETA_ONE) * grad
                )
                second = (
                    BETA_TWO * two[row, rows, lanes].astype(jnp.float32)
                    + (1.0 - BETA_TWO) * (grad * grad)
                )
                root = second * lax.rsqrt(second) + EPSILON * BIAS_TWO**0.5
                new = (1.0 - LEARN_RATE * DECAY_RATE) * master[row, rows, lanes] - (
                    (LEARN_RATE / BIAS_ONE * BIAS_TWO**0.5) * first
                ) / root
                master[row, rows, lanes] = new
                one[row, rows, lanes] = first.astype(jnp.bfloat16)
                two[row, rows, lanes] = second.astype(jnp.bfloat16)
                sums[place, :] = new

        for copy in stores(tile):
            copy.start()

    for part in range(sends):

        def fill(slot, carry):
            outgoing[slot] = sums[pl.ds(next_ref[slot] * pitch, height), :].astype(jnp.bfloat16)
            return carry

        lax.fori_loop(part * send_size, (part + 1) * send_size, fill, 0, unroll=4)
        send(part).start()

    for tile in range(tiles):
        for copy in stores(tile):
            copy.wait()
    for part in range(sends):
        send(part).wait()


def adam_step(holder, fresh, next_map, pieces, master, one, two, sends=4):
    slots, height, _ = pieces.shape
    share, experts, width = master.shape
    tiles = experts // 16
    return pl.pallas_call(
        adam_kernel,
        out_shape=(
            pltpu.HBM(master.shape, jnp.float32),
            pltpu.HBM(one.shape, jnp.bfloat16),
            pltpu.HBM(two.shape, jnp.bfloat16),
            pltpu.HBM((slots, height, LANES), jnp.bfloat16),
        ),
        in_specs=[FAR] * 3 + [NEAR] + [FAR] * 3,
        out_specs=(FAR,) * 4,
        scratch_shapes=[
            pltpu.SMEM((slots,), jnp.int32),
            pltpu.SMEM((slots,), jnp.int32),
            pltpu.SMEM((slots,), jnp.int32),
            pltpu.VMEM((experts * (height + 1), LANES), jnp.float32),
            pltpu.VMEM(master.shape, jnp.float32),
            pltpu.VMEM(one.shape, jnp.bfloat16),
            pltpu.VMEM(two.shape, jnp.bfloat16),
            pltpu.VMEM(pieces.shape, jnp.bfloat16),
            pltpu.SemaphoreType.DMA((3,)),
            pltpu.SemaphoreType.DMA((3, tiles)),
            pltpu.SemaphoreType.DMA((3, tiles)),
            pltpu.SemaphoreType.DMA((sends,)),
        ],
        compiler_params=pltpu.CompilerParams(vmem_limit_bytes=60 << 20),
        name="adam_step",
    )(
        holder, fresh, next_map, pltpu.with_memory_space_constraint(pieces, pltpu.VMEM),
        master, one, two,
    )


def rows_kernel(arrived, out_ref, wholes, tall, out_sem):
    slots, depth, _ = arrived.shape
    width = out_ref.shape[1]
    blocks = width // LANES
    share = depth // blocks
    height = tall.shape[1]
    members = height // share
    parts = out_sem.shape[0]
    part_size = slots // parts

    def store(part):
        span = pl.ds(part * part_size * share, part_size * share)
        return pltpu.make_async_copy(wholes.at[span], out_ref.at[span], out_sem.at[part])

    for part in range(parts):

        @pl.loop(part * part_size // members, (part + 1) * part_size // members)
        def _(group):
            base = pl.multiple_of(group * height, 16)
            for member in range(members):
                chunk = arrived[group * members + member].astype(jnp.float32)
                for block in range(blocks):
                    tall[block, member * share : (member + 1) * share, :] = chunk[
                        block * share : (block + 1) * share, :
                    ]
            for block in range(blocks):
                wholes[pl.ds(base, height), block * LANES : (block + 1) * LANES] = tall[
                    block
                ].astype(jnp.bfloat16)

        store(part).start()
    for part in range(parts):
        store(part).wait()


def chunk_rows(arrived, hidden, width, parts=8, members=8):
    slots, height, _ = arrived.shape
    blocks = width // LANES
    share = height // blocks
    return pl.pallas_call(
        rows_kernel,
        out_shape=jax.ShapeDtypeStruct((hidden, width), jnp.bfloat16),
        in_specs=[NEAR],
        out_specs=FAR,
        scratch_shapes=[
            pltpu.VMEM((hidden, width), jnp.bfloat16),
            pltpu.VMEM((blocks, members * share, LANES), jnp.float32),
            pltpu.SemaphoreType.DMA((parts,)),
        ],
        compiler_params=pltpu.CompilerParams(vmem_limit_bytes=32 << 20),
        name="chunk_rows",
    )(pltpu.with_memory_space_constraint(arrived, pltpu.VMEM))


def exchange(chunks):
    return lax.all_to_all(chunks, "dev", split_axis=0, concat_axis=0, tiled=True)


def per_device(saved, cotangent, weights, counts, live_rows, next_map, master, moment1, moment2):
    cot_rows = cotangent[0]
    devices = lax.axis_size("dev")
    experts, share, width = master.shape
    hidden = saved.shape[2]
    chunks = slot_chunks(saved[0], cot_rows, live_rows, devices)
    received = exchange(chunks)
    input_grads = input_rows(cot_rows, weights[0], live_rows)
    slot_index = jnp.arange(devices, dtype=jnp.int32)
    bounds = jnp.cumsum(counts)
    holders = jnp.sum((bounds[None, :] <= slot_index[:, None]).astype(jnp.int32), axis=1)
    fresh = jnp.any(bounds[None, :] == slot_index[:, None], axis=1) | (slot_index == 0)
    new_master, new_one, new_two, outgoing = adam_step(
        holders, fresh.astype(jnp.int32), next_map, received,
        master.transpose(1, 0, 2), moment1.transpose(1, 0, 2), moment2.transpose(1, 0, 2),
    )
    arriving = exchange(outgoing)
    next_weights = chunk_rows(arriving, hidden, width)
    return (
        input_grads[None],
        new_master.transpose(1, 0, 2),
        new_one.transpose(1, 0, 2),
        new_two.transpose(1, 0, 2),
        next_weights[None],
    )


def solution(mesh):
    placed = (
        P("dev", None, None),
        P("dev", None, None),
        P("dev", None, None),
        P(),
        P("dev"),
        P(),
        P(None, "dev", None),
        P(None, "dev", None),
        P(None, "dev", None),
    )
    return jax.shard_map(
        per_device,
        mesh=mesh,
        in_specs=placed,
        out_specs=(
            P("dev", None, None),
            P(None, "dev", None),
            P(None, "dev", None),
            P(None, "dev", None),
            P("dev", None, None),
        ),
        check_vma=False,
    )
```
